32 devices in a mesh: chan: 4 (over z), tile: 8 (over y, x, core).
Axes of the slice: x: 2, y: 2, z: 4, core: 2. Of those that a mesh axis runs over, the one named last changes fastest.
Arguments:
- visibility: bfloat16 [1024, 2, 1024], P('tile', None, 'chan'), may hold values from -6 to 6
- flags: int32 [1024, 1024], P('tile', 'chan'), may hold values 0 or 1
- u_index: int32 [1024], replicated, may hold values from 0 to 511
- v_index: int32 [1024], replicated, may hold values from 0 to 255
- fg_filter: bfloat16 [1024, 1024], replicated, may hold values from -1 to 1
Outputs:
- cleaned: float32 [1024, 2, 1024], P('tile', None, 'chan')
The draws below stay inside these ranges and needn't reach their ends.
All inputs are finite; a program needn't handle non-finite values. No bound on the sum of `flags` on one device may be relied on, other than what follows from the above.
Results may differ from the reference program's by a relative error of at most 0.0029.
Values may be sent and summed in bfloat16 or wider, within the bound.
No kernel may reach another device: no remote copies, remote signals or barrier semaphores. Data moves between devices by JAX's collectives and lax.ppermute only.
A program may use at most 256 MiB of HBM per device.

```python
import math
import jax
import jax.numpy as jnp
from jax import lax

F = 1024
L = 512
M = 256
ROWS = 1024


def draw_fg_filter(key, part):
    first_key, second_key = jax.random.split(jax.random.fold_in(key, 11))
    spread = jax.random.normal(first_key, (F, F), jnp.float32) * (0.5 / math.sqrt(F))
    diagonal = jax.random.uniform(second_key, (F,), jnp.float32, 0.3, 0.7)
    whole = spread + jnp.eye(F, dtype=jnp.float32) * diagonal[None, :]
    return whole.astype(jnp.bfloat16)


def plant(array, rng, low, largest):
    dims = array.shape
    spot = [jax.random.randint(jax.random.fold_in(rng, axis), (), 0, dims[axis]) for axis in range(len(dims))]
    array = array.at[tuple(spot)].set(low)
    longest = dims.index(max(dims))
    spot[longest] = (spot[longest] + 1) % dims[longest]
    return array.at[tuple(spot)].set(largest)


def block_scale(stream_key, extent, shards, least, largest):
    factor_of, own = 1.0, jax.random.fold_in(stream_key, 6)
    for dim, shards_of in shards:
        steps = jnp.exp(jax.random.uniform(jax.random.fold_in(own, dim), (shards_of,), jnp.float32, least / len(shards), largest / len(shards)))
        factor_of = factor_of * jnp.repeat(steps, extent[dim] // shards_of).reshape([-1 if axis == dim else 1 for axis in range(len(extent))])
    return factor_of


def centred(own_key, shape, deviation, most, shards=(), held_as=jnp.bfloat16):
    array = deviation * jax.random.normal(own_key, shape, jnp.float32)
    if shards:
        array = array * block_scale(own_key, shape, shards, -0.22, 0.18)
    return jnp.clip(array, -most, most).astype(held_as)


def setup_inputs(seed: int = 0) -> dict:
    streams_of = jax.random.split(jax.random.key(seed), 6)
    return {
        "visibility": centred(streams_of[0], (ROWS, 2, F), 1.0, 6.0, ((0, 8), (2, 4))),
        "flags": plant((jax.random.randint(streams_of[1], (ROWS, F), 0, 8) < 7).astype(jnp.int32), jax.random.fold_in(streams_of[1], 1), 0, 1),
        "u_index": plant(jax.random.randint(streams_of[2], (ROWS,), 0, L), jax.random.fold_in(streams_of[2], 1), 0, L - 1).astype(jnp.int32),
        "v_index": plant(jax.random.randint(streams_of[3], (ROWS,), 0, M), jax.random.fold_in(streams_of[3], 1), 0, M - 1).astype(jnp.int32),
        "fg_filter": draw_fg_filter(jax.random.fold_in(streams_of[5], 71), 0),
    }


TWO_PI = 2.0 * math.pi
BLOCK_LINES = 8
FINE_STEP = 8

def tables(grid_index, positions, period):
    turn_count = grid_index[:, None] * positions[None, :] % period
    angles = turn_count.astype(jnp.float32) * (TWO_PI / period)
    return (jnp.cos(angles).astype(jnp.bfloat16), jnp.sin(angles).astype(jnp.bfloat16))

def line_tables(u_rows, line_ids, chan_start, chan_count, chan_total, line_total):
    period = chan_total * line_total
    coarse_ids = chan_total + chan_start + FINE_STEP * jnp.arange(chan_count // FINE_STEP, dtype=jnp.int32)
    fine_ids = jnp.arange(FINE_STEP, dtype=jnp.int32)
    base = u_rows[:, None] * line_ids[None, :]
    coarse_turns = base[:, :, None] * coarse_ids[None, None, :] % period
    fine_turns = base[:, :, None] * fine_ids[None, None, :] % period
    coarse_angle = coarse_turns.astype(jnp.float32) * (TWO_PI / period)
    fine_angle = fine_turns.astype(jnp.float32) * (TWO_PI / period)
    coarse_cos = jnp.cos(coarse_angle)[:, :, :, None]
    coarse_sin = jnp.sin(coarse_angle)[:, :, :, None]
    fine_cos = jnp.cos(fine_angle)[:, :, None, :]
    fine_sin = jnp.sin(fine_angle)[:, :, None, :]
    whole_cos = coarse_cos * fine_cos - coarse_sin * fine_sin
    whole_sin = coarse_sin * fine_cos + coarse_cos * fine_sin
    shape = (u_rows.shape[0], line_ids.shape[0], chan_count)
    return (whole_cos.reshape(shape).astype(jnp.bfloat16), whole_sin.reshape(shape).astype(jnp.bfloat16))

def reference(visibility, flags, u_index, v_index, fg_filter):
    weight = flags.astype(jnp.bfloat16)
    weighted = visibility * weight[:, None, :]
    real_part = weighted[:, 0, :].astype(jnp.float32)[:, None, :]
    imag_part = weighted[:, 1, :].astype(jnp.float32)[:, None, :]
    cos_col, sin_col = tables(v_index, jnp.arange(M, dtype=jnp.int32), 2 * M)
    phase_cols = jnp.concatenate([cos_col, -sin_col], 0)
    phase_both = jnp.concatenate([cos_col, sin_col], 0)
    image_scale = 1.0 / math.sqrt(ROWS)
    filter_wide = fg_filter.astype(jnp.float32)

    def one_block(running, block_index):
        line_ids = block_index * BLOCK_LINES + jnp.arange(BLOCK_LINES, dtype=jnp.int32)
        cos_line, sin_line = line_tables(u_index, line_ids, 0, F, F, L)
        line_cos = cos_line.astype(jnp.float32)
        line_sin = sin_line.astype(jnp.float32)
        x_real = (real_part * line_cos - imag_part * line_sin).astype(jnp.bfloat16)
        x_imag = (real_part * line_sin + imag_part * line_cos).astype(jnp.bfloat16)
        stacked = jnp.concatenate([x_real, x_imag], 0).reshape(2 * ROWS, BLOCK_LINES * F)
        dirty_sum = lax.dot_general(stacked, phase_cols, (((0,), (0,)), ((), ())), preferred_element_type=jnp.float32)
        dirty_image = (dirty_sum * image_scale).astype(jnp.bfloat16).reshape(BLOCK_LINES, F, M)
        foreground = jnp.einsum('fg,qgm->qfm', filter_wide, dirty_image.astype(jnp.float32)).astype(jnp.bfloat16)
        hidden_sum = lax.dot_general(foreground.reshape(BLOCK_LINES * F, M), phase_both, (((1,), (1,)), ((), ())), preferred_element_type=jnp.float32)
        hidden_sum = hidden_sum.reshape(BLOCK_LINES, F, 2, ROWS)
        half_cos = hidden_sum[:, :, 0, :]
        half_sin = hidden_sum[:, :, 1, :]
        row_cos = jnp.transpose(line_cos, (1, 2, 0))
        row_sin = jnp.transpose(line_sin, (1, 2, 0))
        real_pred = lax.optimization_barrier(jnp.sum(row_cos * half_cos - row_sin * half_sin, axis=0))
        imag_pred = -lax.optimization_barrier(jnp.sum(row_sin * half_cos + row_cos * half_sin, axis=0))
        return (running + jnp.stack([real_pred, imag_pred], 0), None)
    initial = jnp.zeros((2, F, ROWS), jnp.float32)
    summed, _ = lax.scan(one_block, initial, jnp.arange(L // BLOCK_LINES, dtype=jnp.int32))
    predicted = jnp.transpose(summed, (2, 0, 1)) * (1.0 / math.sqrt(L * M))
    return weight.astype(jnp.float32)[:, None, :] * (visibility.astype(jnp.float32) - predicted)
```

```python
import functools
import math

import jax
import jax.numpy as jnp
import numpy as np
from jax import lax
from jax.experimental import pallas as pl
from jax.experimental.pallas import tpu as pltpu
from jax.sharding import PartitionSpec as P

F = 1024
L = 512
M = 256

TWO_PI = 2.0 * math.pi
FINE = 8
LANES = 128
A_CHANS = 16
C_CHANS = 16
F32 = jnp.float32
BF16 = jnp.bfloat16


def tile_masks(tiles):
    bits = [1 << i for i in range(1, tiles.bit_length() - 1)]
    swapped = bits[1::-1] + bits[2:]
    return (bits, swapped)


def block_order(tiles):
    offsets = []
    for masks in tile_masks(tiles):
        held = [0]
        for mask in masks:
            held = held + [s ^ mask for s in held]
        offsets.append(held)
    rows = []
    for t in range(tiles):
        own = [t ^ s for s in offsets[t & 1]]
        rows.append(own + [(t ^ 1) ^ s for s in offsets[1 - (t & 1)]])
    return np.asarray(rows, np.int32)


def stage_pairs(tiles, stage):
    even, odd = tile_masks(tiles)
    return [(t, t ^ (odd if t & 1 else even)[stage]) for t in range(tiles)]


def gather_tile(block, tiles):
    held = block[None]
    for stage in range(len(tile_masks(tiles)[0])):
        held = jnp.concatenate([held, lax.ppermute(held, "tile", stage_pairs(tiles, stage))], 0)
    other = lax.ppermute(held, "tile", [(t, t ^ 1) for t in range(tiles)])
    return jnp.concatenate([held, other], 0)


def reduce_tile(kept, sent, tiles):
    received = lax.ppermute(sent, "tile", [(t, t ^ 1) for t in range(tiles)])
    total = kept + received.astype(F32)
    for stage in reversed(range(len(tile_masks(tiles)[0]))):
        half = total.shape[0] // 2
        received = lax.ppermute(total[half:].astype(BF16), "tile", stage_pairs(tiles, stage))
        total = total[:half] + received.astype(F32)
    return total[0]


def unit(turns, period):
    angle = (turns % period).astype(F32) * (TWO_PI / period)
    return jnp.cos(angle), jnp.sin(angle)


def times(a, b):
    return a[0] * b[0] - a[1] * b[1], a[1] * b[0] + a[0] * b[1]


def column_tables(v_rows):
    digit = 16
    high = unit(v_rows[None, :] * (digit * jnp.arange(M // digit, dtype=jnp.int32))[:, None], 2 * M)
    low = unit(v_rows[None, :] * jnp.arange(digit, dtype=jnp.int32)[:, None], 2 * M)
    both = times(
        (high[0][:, None, :], high[1][:, None, :]), (low[0][None, :, :], low[1][None, :, :])
    )
    return [part.reshape(M, -1).astype(BF16) for part in both]


def phase_tables(scaled_rows, period):
    groups = F // FINE
    digit = 16
    high_ids = F + FINE * digit * jnp.arange(groups // digit, dtype=jnp.int32)
    high = unit(scaled_rows[None, :] * high_ids[:, None], period)
    low = unit(
        scaled_rows[None, :] * (FINE * jnp.arange(digit, dtype=jnp.int32))[:, None], period
    )
    coarse = times(
        (high[0][:, None, :], high[1][:, None, :]), (low[0][None, :, :], low[1][None, :, :])
    )
    fine = unit(scaled_rows[None, :] * jnp.arange(FINE, dtype=jnp.int32)[:, None], period)
    coarse = jnp.stack([part.reshape(groups, -1, LANES) for part in coarse])
    return jnp.transpose(coarse, (0, 2, 1, 3)), jnp.stack(fine)


def phases(coarse_ref, fine_ref, group, chans, block):
    lanes = slice(block * LANES, (block + 1) * LANES)
    fine = (fine_ref[0, :, lanes], fine_ref[1, :, lanes])
    parts = []
    for step in range(chans // FINE):
        row = pl.ds(group + step, FINE, stride=0)
        coarse = (coarse_ref[0, block, row, :], coarse_ref[1, block, row, :])
        parts.append(times(coarse, fine))
    return (
        jnp.concatenate([part[0] for part in parts], 0),
        jnp.concatenate([part[1] for part in parts], 0),
    )


def paired(count, first, second):
    first(0, 0)

    def body(pair, carry):
        first(2 * pair + 1, 1)
        second(2 * pair, 0)
        first(2 * pair + 2, 0)
        second(2 * pair + 1, 1)
        return carry

    lax.fori_loop(0, count // 2 - 1, body, 0)
    first(count - 1, 1)
    second(count - 2, 0)
    second(count - 1, 1)


def image_kernel(scale, lines, place_ref, vis_ref, step_c, step_f, start_c, start_f, col_ref, out_ref, x0, x1):
    blocks, _, chans, _ = vis_ref.shape
    base = place_ref[0]
    slots = (x0, x1)

    def fill(i, slot):
        x_ref = slots[slot]
        rows = pl.ds(pl.multiple_of(i * A_CHANS, A_CHANS), A_CHANS)
        group = base + i * (A_CHANS // FINE)
        for block in range(blocks):
            step = phases(step_c, step_f, group, A_CHANS, block)
            start = phases(start_c, start_f, group, A_CHANS, block)
            value = (vis_ref[block, 0, rows, :].astype(F32), vis_ref[block, 1, rows, :].astype(F32))
            value = times(value, start)
            at = block * 2 * LANES
            for line in range(lines):
                into = slice(line * A_CHANS, (line + 1) * A_CHANS)
                x_ref[into, at : at + LANES] = value[0].astype(BF16)
                x_ref[into, at + LANES : at + 2 * LANES] = value[1].astype(BF16)
                if line < lines - 1:
                    value = times(value, step)

    def multiply(i, slot):
        rows = pl.ds(pl.multiple_of(i * A_CHANS, A_CHANS), A_CHANS)
        image = jnp.dot(slots[slot][...], col_ref[...], preferred_element_type=F32) * scale
        out_ref[:, rows, :] = image.astype(BF16).reshape(lines, A_CHANS, M)

    paired(chans // A_CHANS, fill, multiply)


def make_image(vis, place, step_t, start_t, col, lines, total_rows):
    blocks, _, chans, _ = vis.shape
    rows = blocks * LANES
    vmem = pl.BlockSpec(memory_space=pltpu.VMEM)
    flops = 2 * lines * chans * 2 * rows * M
    return pl.pallas_call(
        functools.partial(image_kernel, 1.0 / math.sqrt(total_rows), lines),
        out_shape=jax.ShapeDtypeStruct((lines, chans, M), BF16),
        in_specs=[pl.BlockSpec(memory_space=pltpu.SMEM)] + [vmem] * 6,
        out_specs=vmem,
        scratch_shapes=[pltpu.VMEM((lines * A_CHANS, 2 * rows), BF16)] * 2,
        compiler_params=pltpu.CompilerParams(vmem_limit_bytes=40 << 20),
        cost_estimate=pl.CostEstimate(flops=flops, bytes_accessed=8 << 20, transcendentals=0),
        name="image",
    )(place, vis, *step_t, *start_t, col)


def filter_kernel(groups, chans, place_ref, filter_ref, *refs):
    image_refs, out_ref = refs[:groups], refs[groups]
    lines = out_ref.shape[0]
    place = place_ref[0]
    whole = []
    for out_block in range(groups):
        rows = pl.ds(pl.multiple_of(lax.rem(place + out_block, groups) * chans, chans), chans)
        pieces = []
        for in_block in range(groups):
            at = lax.rem(place + (groups - in_block), groups) * chans
            pieces.append(filter_ref[rows, pl.ds(pl.multiple_of(at, chans), chans)])
        whole.append(jnp.concatenate(pieces, 1))
    weights = jnp.concatenate(whole, 0)
    image = jnp.concatenate(
        [jnp.concatenate([ref[line] for line in range(lines)], 1) for ref in image_refs], 0
    )
    result = jnp.dot(weights, image, preferred_element_type=F32).astype(BF16)
    for line in range(lines):
        out_ref[line] = result[:, line * M : (line + 1) * M]


def filter_images(images, place, fg_filter):
    groups = len(images)
    lines, chans, _ = images[0].shape
    step = min(4, lines)
    return pl.pallas_call(
        functools.partial(filter_kernel, groups, chans),
        out_shape=jax.ShapeDtypeStruct((lines, F, M), BF16),
        grid=(lines // step,),
        in_specs=[
            pl.BlockSpec(memory_space=pltpu.SMEM),
            pl.BlockSpec((F, F), lambda i: (0, 0), pipeline_mode=pl.Buffered(1)),
        ]
        + [pl.BlockSpec((step, chans, M), lambda i: (i, 0, 0))] * groups,
        out_specs=pl.BlockSpec((step, F, M), lambda i: (i, 0, 0)),
        compiler_params=pltpu.CompilerParams(vmem_limit_bytes=40 << 20),
        cost_estimate=pl.CostEstimate(
            flops=2 * F * F * lines * M, bytes_accessed=18 << 20, transcendentals=0
        ),
        name="filter",
    )(place, fg_filter, *images)


def predict_kernel(scale, place_ref, image_ref, col_ref, step_c, step_f, start_c, start_f, keep_ref, send_ref, h0, h1):
    lines, chans, _ = image_ref.shape
    blocks = 2 * keep_ref.shape[0]
    base = place_ref[0]
    slots = (h0, h1)

    def multiply(i, slot):
        rows = pl.ds(pl.multiple_of(i * C_CHANS, C_CHANS), C_CHANS)
        image = image_ref[:, rows, :].reshape(lines * C_CHANS, M)
        slots[slot][...] = jnp.dot(image, col_ref[...], preferred_element_type=F32)

    def collect(i, slot):
        h_ref = slots[slot]
        rows = pl.ds(pl.multiple_of(i * C_CHANS, C_CHANS), C_CHANS)
        group = base + i * (C_CHANS // FINE)
        for block in range(blocks):
            step = phases(step_c, step_f, group, C_CHANS, block)
            start = phases(start_c, start_f, group, C_CHANS, block)
            at = block * 2 * LANES
            total = None
            for line in reversed(range(lines)):
                take = slice(line * C_CHANS, (line + 1) * C_CHANS)
                value = (h_ref[take, at : at + LANES], h_ref[take, at + LANES : at + 2 * LANES])
                if total is None:
                    total = value
                else:
                    moved = times(total, step)
                    total = (moved[0] + value[0], moved[1] + value[1])
            total = times(total, start)
            if block < blocks // 2:
                keep_ref[block, 0, rows, :] = total[0] * scale
                keep_ref[block, 1, rows, :] = total[1] * -scale
            else:
                send_ref[block - blocks // 2, 0, rows, :] = (total[0] * scale).astype(BF16)
                send_ref[block - blocks // 2, 1, rows, :] = (total[1] * -scale).astype(BF16)

    paired(chans // C_CHANS, multiply, collect)


def predict_part(foreground, index, place, step_t, start_t, col, chans):
    lines = foreground.shape[0]
    rows = col.shape[1] // 2
    blocks = rows // LANES
    vmem = pl.BlockSpec(memory_space=pltpu.VMEM)
    flops = 2 * lines * chans * 2 * rows * M
    half = (blocks // 2, 2, chans, LANES)
    whole = lambda *shape: pl.BlockSpec(shape, lambda i: (0,) * len(shape), pipeline_mode=pl.Buffered(1))
    return pl.pallas_call(
        functools.partial(predict_kernel, 1.0 / math.sqrt(L * M)),
        out_shape=(jax.ShapeDtypeStruct(half, F32), jax.ShapeDtypeStruct(half, BF16)),
        grid=(1,),
        in_specs=[
            pl.BlockSpec(memory_space=pltpu.SMEM),
            pl.BlockSpec((lines, chans, M), lambda i: (0, index, 0), pipeline_mode=pl.Buffered(1)),
        ]
        + [whole(*a.shape) for a in (col, *step_t, *start_t)],
        out_specs=(whole(*half), whole(*half)),
        scratch_shapes=[pltpu.VMEM((lines * C_CHANS, 2 * rows), F32)] * 2,
        compiler_params=pltpu.CompilerParams(vmem_limit_bytes=40 << 20),
        cost_estimate=pl.CostEstimate(flops=flops, bytes_accessed=8 << 20, transcendentals=0),
        name="predict",
    )(place, foreground, col, *step_t, *start_t)


def local(visibility, flags, u_index, v_index, fg_filter):
    groups, tiles = lax.axis_size("chan"), lax.axis_size("tile")
    chan, tile = lax.axis_index("chan"), lax.axis_index("tile")
    chans = visibility.shape[2]
    total_rows = u_index.shape[0]
    lines = L // (groups * tiles)
    period = F * L

    weight = flags.astype(BF16)
    own = jnp.transpose(visibility * weight[:, None, :], (1, 2, 0))
    seen = [own]
    for away in range(1, groups):
        seen.append(
            lax.ppermute(own, "chan", [(c, (c + away) % groups) for c in range(groups)])
        )
    seen = [gather_tile(block, tiles) for block in seen]

    order = lax.dynamic_index_in_dim(jnp.asarray(block_order(tiles)), tile, 0, keepdims=False)
    u_rows = u_index.reshape(tiles, LANES)[order].reshape(-1)
    v_rows = v_index.reshape(tiles, LANES)[order].reshape(-1)
    first_line = (chan * tiles + tile) * lines
    step_t = phase_tables(u_rows, period)
    start_t = phase_tables(u_rows * first_line, period)
    cos_col, sin_col = column_tables(v_rows)
    predict_col = jnp.stack(
        [cos_col.reshape(M, tiles, LANES), sin_col.reshape(M, tiles, LANES)], 2
    ).reshape(M, 2 * total_rows)
    image_col = jnp.stack(
        [cos_col.T.reshape(tiles, LANES, M), -sin_col.T.reshape(tiles, LANES, M)], 1
    ).reshape(2 * total_rows, M)

    images = []
    for away, block in enumerate(seen):
        place = (lax.rem(chan + groups - away, groups) * (chans // FINE)).reshape(1)
        images.append(make_image(block, place, step_t, start_t, image_col, lines, total_rows))
    foreground = filter_images(images, chan.reshape(1), fg_filter)

    parts = []
    for away in list(range(1, groups)) + [0]:
        place = (lax.rem(chan + away, groups) * (chans // FINE)).reshape(1)
        kept, sent = predict_part(foreground, away, place, step_t, start_t, predict_col, chans)
        part = reduce_tile(kept, sent, tiles)
        if away:
            part = lax.ppermute(
                part.astype(BF16), "chan", [(c, (c + away) % groups) for c in range(groups)]
            ).astype(F32)
        parts.append(part)
    predicted = jnp.transpose(functools.reduce(jnp.add, parts), (2, 0, 1))
    return weight.astype(F32)[:, None, :] * (visibility.astype(F32) - predicted)


def solution(mesh):
    return jax.shard_map(
        local,
        mesh=mesh,
        in_specs=(P("tile", None, "chan"), P("tile", "chan"), P(), P(), P()),
        out_specs=P("tile", None, "chan"),
        check_vma=False,
    )
```

```python
import functools
import math

import jax
import jax.numpy as jnp
import numpy as np
from jax import lax
from jax.experimental import pallas as pl
from jax.experimental.pallas import tpu as pltpu
from jax.sharding import PartitionSpec as P

F = 1024
L = 512
M = 256

TWO_PI = 2.0 * math.pi
FINE = 8
LANES = 128
A_CHANS = 16
C_CHANS = 64
C_UNIT = 16
C_SLOTS = 2
F32 = jnp.float32
BF16 = jnp.bfloat16


def chip_masks(tiles):
    return [mask for mask in range(0, tiles, 2)]


def tile_swap(block, tiles, mask):
    return lax.ppermute(block, "tile", [(t, t ^ mask) for t in range(tiles)])


def chan_shift(block, groups, away):
    return lax.ppermute(block, "chan", [(c, (c + away) % groups) for c in range(groups)])


def after(value, *others):
    return lax.optimization_barrier((value, *others))[0]


def unit(turns, period):
    angle = (turns % period).astype(F32) * (TWO_PI / period)
    return jnp.cos(angle), jnp.sin(angle)


def times(a, b):
    return a[0] * b[0] - a[1] * b[1], a[1] * b[0] + a[0] * b[1]


def conj_times(a, b):
    return a[0] * b[0] + a[1] * b[1], a[1] * b[0] - a[0] * b[1]


def column_tables(v_rows):
    digit = 16
    high = unit(v_rows[None, :] * (digit * jnp.arange(M // digit, dtype=jnp.int32))[:, None], 2 * M)
    low = unit(v_rows[None, :] * jnp.arange(digit, dtype=jnp.int32)[:, None], 2 * M)
    both = times(
        (high[0][:, None, :], high[1][:, None, :]), (low[0][None, :, :], low[1][None, :, :])
    )
    return [part.reshape(M, -1).astype(BF16) for part in both]


def phase_tables(scaled_rows, period):
    groups = F // FINE
    digit = 16
    high_ids = F + FINE * digit * jnp.arange(groups // digit, dtype=jnp.int32)
    high = unit(scaled_rows[None, :] * high_ids[:, None], period)
    low = unit(
        scaled_rows[None, :] * (FINE * jnp.arange(digit, dtype=jnp.int32))[:, None], period
    )
    coarse = times(
        (high[0][:, None, :], high[1][:, None, :]), (low[0][None, :, :], low[1][None, :, :])
    )
    fine = unit(scaled_rows[None, :] * jnp.arange(FINE, dtype=jnp.int32)[:, None], period)
    coarse = jnp.stack([part.reshape(groups, -1, LANES) for part in coarse])
    fine = jnp.stack([part.reshape(FINE, -1, LANES) for part in fine])
    return jnp.transpose(coarse, (0, 2, 1, 3)), jnp.transpose(fine, (0, 2, 1, 3))


def phases(coarse_ref, fine_ref, group, chans, block):
    fine = (fine_ref[0, block], fine_ref[1, block])
    parts = []
    for step in range(chans // FINE):
        row = pl.ds(group + step, FINE, stride=0)
        coarse = (coarse_ref[0, block, row, :], coarse_ref[1, block, row, :])
        parts.append(times(coarse, fine))
    return (
        jnp.concatenate([part[0] for part in parts], 0),
        jnp.concatenate([part[1] for part in parts], 0),
    )


def paired(count, first, second):
    first(0, 0)

    def body(pair, carry):
        first(2 * pair + 1, 1)
        second(2 * pair, 0)
        first(jnp.minimum(2 * pair + 2, count - 1), 0)
        second(2 * pair + 1, 1)
        return carry

    lax.fori_loop(0, count // 2, body, 0)


def image_kernel(scale, lines, blocks, place_ref, step_c, step_f, start_c, start_f, col_ref, *refs):
    vis_refs, out_ref, slots = refs[:blocks], refs[blocks], refs[blocks + 1 :]
    chans = out_ref.shape[1]
    base = place_ref[0]

    def fill(i, slot):
        x_ref = slots[slot]
        rows = pl.ds(pl.multiple_of(i * A_CHANS, A_CHANS), A_CHANS)
        group = base + i * (A_CHANS // FINE)
        for block in range(blocks):
            step = phases(step_c, step_f, group, A_CHANS, block)
            start = phases(start_c, start_f, group, A_CHANS, block)
            vis_ref = vis_refs[block]
            value = conj_times((vis_ref[0, rows, :].astype(F32), -vis_ref[1, rows, :].astype(F32)), start)
            at = block * 2 * LANES
            for line in range(lines):
                into = slice(line * A_CHANS, (line + 1) * A_CHANS)
                x_ref[into, at : at + LANES] = value[0].astype(BF16)
                x_ref[into, at + LANES : at + 2 * LANES] = value[1].astype(BF16)
                if line < lines - 1:
                    value = conj_times(value, step)

    def multiply(i, slot):
        rows = pl.ds(pl.multiple_of(i * A_CHANS, A_CHANS), A_CHANS)
        image = jnp.dot(slots[slot][...], col_ref[...], preferred_element_type=F32)
        out_ref[:, rows, :] = (image * scale).astype(BF16).reshape(lines, A_CHANS, M)

    paired(chans // A_CHANS, fill, multiply)


def make_image(vis, place, step_t, start_t, col, lines, total_rows):
    blocks = len(vis)
    _, chans, _ = vis[0].shape
    rows = blocks * LANES
    vmem = pl.BlockSpec(memory_space=pltpu.VMEM)
    flops = 2 * lines * chans * 2 * rows * M
    return pl.pallas_call(
        functools.partial(image_kernel, 1.0 / math.sqrt(total_rows), lines, blocks),
        out_shape=jax.ShapeDtypeStruct((lines, chans, M), BF16),
        in_specs=[pl.BlockSpec(memory_space=pltpu.SMEM)] + [vmem] * (5 + blocks),
        out_specs=vmem,
        scratch_shapes=[pltpu.VMEM((lines * A_CHANS, 2 * rows), BF16)] * 2,
        compiler_params=pltpu.CompilerParams(vmem_limit_bytes=40 << 20),
        cost_estimate=pl.CostEstimate(flops=flops, bytes_accessed=8 << 20, transcendentals=0),
        name="image",
    )(place, *step_t, *start_t, col, *vis)


def filter_kernel(groups, chans, place_ref, filter_ref, *refs):
    image_refs, out_refs = refs[:groups], refs[groups:]
    lines = out_refs[0].shape[0]
    place = place_ref[0]
    whole = []
    for out_block in range(groups):
        rows = pl.ds(pl.multiple_of(lax.rem(place + out_block, groups) * chans, chans), chans)
        pieces = []
        for in_block in range(groups):
            at = lax.rem(place + (groups - in_block), groups) * chans
            pieces.append(filter_ref[rows, pl.ds(pl.multiple_of(at, chans), chans)])
        whole.append(jnp.concatenate(pieces, 1))
    weights = jnp.concatenate(whole, 0)
    image = jnp.concatenate(
        [jnp.concatenate([ref[line] for line in range(lines)], 1) for ref in image_refs], 0
    )
    result = jnp.dot(weights, image, preferred_element_type=F32).astype(BF16)
    for block, out_ref in enumerate(out_refs):
        for line in range(lines):
            out_ref[line] = result[block * chans : (block + 1) * chans, line * M : (line + 1) * M]


def filter_images(images, place, fg_filter):
    groups = len(images)
    lines, chans, _ = images[0].shape
    step = min(4, lines)
    return pl.pallas_call(
        functools.partial(filter_kernel, groups, chans),
        out_shape=[jax.ShapeDtypeStruct((lines, chans, M), BF16)] * groups,
        grid=(lines // step,),
        in_specs=[
            pl.BlockSpec(memory_space=pltpu.SMEM),
            pl.BlockSpec((F, F), lambda i: (0, 0), pipeline_mode=pl.Buffered(1)),
        ]
        + [pl.BlockSpec((step, chans, M), lambda i: (i, 0, 0))] * groups,
        out_specs=[pl.BlockSpec((step, chans, M), lambda i: (i, 0, 0))] * groups,
        compiler_params=pltpu.CompilerParams(vmem_limit_bytes=40 << 20),
        cost_estimate=pl.CostEstimate(
            flops=2 * F * F * lines * M, bytes_accessed=18 << 20, transcendentals=0
        ),
        name="filter",
    )(place, fg_filter, *images)


def predict_kernel(scale, place_ref, image_ref, col_ref, step_c, step_f, start_c, start_f, keep_ref, send_ref, *slots):
    lines, chans, _ = image_ref.shape
    blocks = 2 * keep_ref.shape[0]
    count = chans // C_CHANS
    base = place_ref[0]

    def rows_of(i):
        return pl.ds(pl.multiple_of(i * C_CHANS, C_CHANS), C_CHANS)

    def multiply(i, slot, block):
        image = image_ref[:, rows_of(i), :].reshape(lines * C_CHANS, M)
        at = slice(block * 2 * LANES, (block + 1) * 2 * LANES)
        slots[slot][...] = jnp.dot(image, col_ref[:, at], preferred_element_type=F32)

    def collect(i, slot, block):
        h_ref = slots[slot]
        rows = rows_of(i)
        for first in range(0, C_CHANS, C_UNIT):
            group = base + i * (C_CHANS // FINE) + first // FINE
            step = phases(step_c, step_f, group, C_UNIT, block)
            start = phases(start_c, start_f, group, C_UNIT, block)
            total = None
            for line in reversed(range(lines)):
                take = slice(line * C_CHANS + first, line * C_CHANS + first + C_UNIT)
                value = (h_ref[take, :LANES], h_ref[take, LANES:])
                if total is None:
                    total = value
                else:
                    moved = times(total, step)
                    total = (moved[0] + value[0], moved[1] + value[1])
            total = times(total, start)
            real, imag = total[0] * scale, total[1] * -scale
            into = pl.ds(pl.multiple_of(i * C_CHANS + first, C_UNIT), C_UNIT)
            if block < blocks // 2:
                keep_ref[block, 0, into, :] = real
                keep_ref[block, 1, into, :] = imag
            else:
                send_ref[block - blocks // 2, 0, into, :] = real.astype(BF16)
                send_ref[block - blocks // 2, 1, into, :] = imag.astype(BF16)

    def body(i, carry):
        for block in range(blocks):
            if block < blocks - 1:
                multiply(i, (block + 1) % len(slots), block + 1)
            else:
                multiply(jnp.minimum(i + 1, count - 1), 0, 0)
            collect(i, block % len(slots), block)
        return carry

    multiply(0, 0, 0)
    lax.fori_loop(0, count, body, 0)


def predict_part(foreground, place, step_t, start_t, col):
    lines, chans, _ = foreground.shape
    rows = col.shape[1] // 2
    vmem = pl.BlockSpec(memory_space=pltpu.VMEM)
    flops = 2 * lines * chans * 2 * rows * M
    half = (rows // LANES // 2, 2, chans, LANES)
    return pl.pallas_call(
        functools.partial(predict_kernel, 1.0 / math.sqrt(L * M)),
        out_shape=(jax.ShapeDtypeStruct(half, F32), jax.ShapeDtypeStruct(half, BF16)),
        in_specs=[pl.BlockSpec(memory_space=pltpu.SMEM)] + [vmem] * 6,
        out_specs=(vmem, vmem),
        scratch_shapes=[pltpu.VMEM((lines * C_CHANS, 2 * LANES), F32)] * C_SLOTS,
        compiler_params=pltpu.CompilerParams(vmem_limit_bytes=40 << 20),
        cost_estimate=pl.CostEstimate(flops=flops, bytes_accessed=8 << 20, transcendentals=0),
        name="predict",
    )(place, foreground, col, *step_t, *start_t)


def turn_kernel(col_ref, out_ref):
    for at in range(0, col_ref.shape[1], 2 * LANES):
        out_ref[at : at + 2 * LANES, :] = col_ref[:, at : at + 2 * LANES].T


def turned(col):
    vmem = pl.BlockSpec(memory_space=pltpu.VMEM)
    return pl.pallas_call(
        turn_kernel,
        out_shape=jax.ShapeDtypeStruct(col.shape[::-1], col.dtype),
        in_specs=[vmem],
        out_specs=vmem,
        cost_estimate=pl.CostEstimate(flops=1 << 20, bytes_accessed=2 << 20, transcendentals=0),
        name="turn",
    )(col)


def local(visibility, flags, u_index, v_index, fg_filter):
    groups, tiles = lax.axis_size("chan"), lax.axis_size("tile")
    chan, tile = lax.axis_index("chan"), lax.axis_index("tile")
    chans = visibility.shape[2]
    total_rows = u_index.shape[0]
    lines = L // (groups * tiles)
    period = F * L
    masks = chip_masks(tiles)

    weight = flags.astype(BF16)
    own = jnp.transpose(visibility * weight[:, None, :], (1, 2, 0))
    seen = [own] + [chan_shift(own, groups, away) for away in range(1, groups)]
    near, far = [], []
    for away in range(groups):
        block = seen[away] if away < 2 else after(seen[away], *near[away - 2][1:])
        near.append([block] + [tile_swap(block, tiles, mask) for mask in masks[1:]])
        far.append([tile_swap(piece, tiles, 1) for piece in near[away]])

    order = tile ^ jnp.asarray(np.asarray(masks + [mask ^ 1 for mask in masks], np.int32))
    u_rows = u_index.reshape(tiles, LANES)[order].reshape(-1)
    v_rows = v_index.reshape(tiles, LANES)[order].reshape(-1)
    first_line = (chan * tiles + tile) * lines
    step_t = phase_tables(u_rows, period)
    start_t = phase_tables(u_rows * first_line, period)
    cos_col, sin_col = column_tables(v_rows)
    predict_col = jnp.stack(
        [cos_col.reshape(M, tiles, LANES), sin_col.reshape(M, tiles, LANES)], 2
    ).reshape(M, 2 * total_rows)
    image_col = turned(predict_col)

    images = []
    for away in range(groups):
        place = (lax.rem(chan + groups - away, groups) * (chans // FINE)).reshape(1)
        if away + 1 < groups:
            place = after(place, *near[away + 1][1:])
        blocks = near[away] + far[away]
        images.append(make_image(blocks, place, step_t, start_t, image_col, lines, total_rows))
    foreground = filter_images(images, chan.reshape(1), fg_filter)

    parts, first_halves, second_halves = [], [], []
    for turn, away in enumerate(list(range(1, groups)) + [0]):
        place = (lax.rem(chan + away, groups) * (chans // FINE)).reshape(1)
        if turn >= 2:
            place = after(place, first_halves[turn - 2])
        if turn >= 3:
            place = after(place, *second_halves[turn - 3])
        kept, sent = predict_part(foreground[away], place, step_t, start_t, predict_col)
        received = tile_swap(sent, tiles, 1)
        first_halves.append(received)
        total = kept + received.astype(F32)
        received = [
            tile_swap(total[spot].astype(BF16), tiles, mask)
            for spot, mask in enumerate(masks)
            if mask
        ]
        second_halves.append(received)
        part = total[0] + functools.reduce(jnp.add, [piece.astype(F32) for piece in received])
        if away:
            part = chan_shift(part.astype(BF16), groups, away).astype(F32)
        parts.append(part)
    predicted = jnp.transpose(functools.reduce(jnp.add, parts), (2, 0, 1))
    return weight.astype(F32)[:, None, :] * (visibility.astype(F32) - predicted)


def solution(mesh):
    return jax.shard_map(
        local,
        mesh=mesh,
        in_specs=(P("tile", None, "chan"), P("tile", "chan"), P(), P(), P()),
        out_specs=P("tile", None, "chan"),
        check_vma=False,
    )
```

```python
import functools
import math

import jax
import jax.numpy as jnp
from jax import lax
from jax.experimental import pallas as pl
from jax.experimental.pallas import tpu as pltpu
from jax.sharding import PartitionSpec as P

F = 1024
L = 512
M = 256

TWO_PI = 2.0 * math.pi
FINE = 8
DIGIT = 16
GROUPS = F // FINE
TOKEN = jax.ShapeDtypeStruct((1,), jnp.int32)
LANES = 128
A_CHANS = 16
C_CHANS = 64
C_UNIT = 16
C_SLOTS = 2
VMEM_SMALL = 8 << 20
VMEM_FILTER = 16 << 20
F32 = jnp.float32
BF16 = jnp.bfloat16


def chip_masks(tiles):
    return [mask for mask in range(0, tiles, 2)]


def tile_swap(block, tiles, mask):
    return lax.ppermute(block, "tile", [(t, t ^ mask) for t in range(tiles)])


def chan_shift(block, groups, away):
    return lax.ppermute(block, "chan", [(c, (c + away) % groups) for c in range(groups)])


def after(value, *others):
    return lax.optimization_barrier((value, *others))[0]


def times(a, b):
    return a[0] * b[0] - a[1] * b[1], a[1] * b[0] + a[0] * b[1]


def conj_times(a, b):
    return a[0] * b[0] + a[1] * b[1], a[1] * b[0] - a[0] * b[1]


def turn_unit(turns, period):
    angle = (turns & (period - 1)).astype(F32) * (TWO_PI / period)
    return jnp.cos(angle), jnp.sin(angle)


def row_of(pair, row, height):
    return tuple(jnp.broadcast_to(part[row : row + 1], (height, LANES)) for part in pair)


def table_kernel(tiles, place_ref, u_ref, v_ref, step_ref, start_ref, col_ref, turned_ref, token_ref):
    tile, first_line = place_ref[0], place_ref[1]
    ids = lax.broadcasted_iota(jnp.int32, (DIGIT, LANES), 0)
    token_ref[0] = tile
    masks = chip_masks(tiles)
    for block, mask in enumerate(masks + [mask ^ 1 for mask in masks]):
        source = pl.ds(tile ^ mask, FINE, stride=0)
        u_row, v_row = u_ref[source, :], v_ref[source, :]
        for scaled, table_ref in ((u_row, step_ref), (u_row * first_line, start_ref)):
            deep = jnp.concatenate([scaled] * (DIGIT // FINE), 0)
            high = turn_unit(deep * (F + FINE * DIGIT * ids), F * L)
            low = turn_unit(deep * (FINE * ids), F * L)
            fine = turn_unit(scaled * ids[:FINE], F * L)
            for row in range(GROUPS // DIGIT):
                both = times(row_of(high, row, DIGIT), low)
                for part in range(2):
                    table_ref[part, block, row * DIGIT : (row + 1) * DIGIT, :] = both[part]
            for part in range(2):
                table_ref[part, block, GROUPS:, :] = fine[part]
        deep = jnp.concatenate([v_row] * (DIGIT // FINE), 0)
        high = turn_unit(deep * (DIGIT * ids), 2 * M)
        low = turn_unit(deep * ids, 2 * M)
        rows = []
        for row in range(M // DIGIT):
            both = times(row_of(high, row, DIGIT), low)
            rows.append(jnp.concatenate(both, 1).astype(BF16))
        at = slice(block * 2 * LANES, (block + 1) * 2 * LANES)
        whole = jnp.concatenate(rows, 0)
        col_ref[:, at] = whole
        turned_ref[at, :] = whole.T


def tables(u_index, v_index, place, tiles):
    rows = u_index.shape[0]
    vmem = pl.BlockSpec(memory_space=pltpu.VMEM)
    digits = jax.ShapeDtypeStruct((2, tiles, GROUPS + FINE, LANES), F32)
    return pl.pallas_call(
        functools.partial(table_kernel, tiles),
        out_shape=(
            digits,
            digits,
            jax.ShapeDtypeStruct((M, 2 * rows), BF16),
            jax.ShapeDtypeStruct((2 * rows, M), BF16),
            TOKEN,
        ),
        in_specs=[pl.BlockSpec(memory_space=pltpu.SMEM), vmem, vmem],
        out_specs=(vmem,) * 4 + (pl.BlockSpec(memory_space=pltpu.SMEM),),
        compiler_params=pltpu.CompilerParams(vmem_limit_bytes=VMEM_SMALL),
        cost_estimate=pl.CostEstimate(flops=1 << 24, bytes_accessed=4 << 20, transcendentals=1 << 18),
        name="tables",
    )(place, u_index.reshape(tiles, LANES), v_index.reshape(tiles, LANES))


def phases(table_ref, group, chans, block):
    fine = (table_ref[0, block, GROUPS:, :], table_ref[1, block, GROUPS:, :])
    parts = []
    for step in range(chans // FINE):
        rows = pl.ds(group + step, FINE, stride=0)
        parts.append(times((table_ref[0, block, rows, :], table_ref[1, block, rows, :]), fine))
    return (
        jnp.concatenate([part[0] for part in parts], 0),
        jnp.concatenate([part[1] for part in parts], 0),
    )


def paired(count, first, second):
    first(0, 0)

    def body(pair, carry):
        first(2 * pair + 1, 1)
        second(2 * pair, 0)
        first(jnp.minimum(2 * pair + 2, count - 1), 0)
        second(2 * pair + 1, 1)
        return carry

    lax.fori_loop(0, count // 2, body, 0)


def image_kernel(scale, lines, blocks, groups, away, place_ref, step_ref, start_ref, col_ref, *refs):
    vis_refs, (out_ref, token_ref), slots = refs[:blocks], refs[blocks : blocks + 2], refs[blocks + 2 :]
    token_ref[0] = place_ref[0]
    chans = out_ref.shape[1]
    base = lax.rem(place_ref[2] + groups - away, groups) * (chans // FINE)

    def fill(i, slot):
        x_ref = slots[slot]
        rows = pl.ds(pl.multiple_of(i * A_CHANS, A_CHANS), A_CHANS)
        group = base + i * (A_CHANS // FINE)
        for block in range(blocks):
            step = phases(step_ref, group, A_CHANS, block)
            start = phases(start_ref, group, A_CHANS, block)
            vis_ref = vis_refs[block]
            value = conj_times((vis_ref[0, rows, :].astype(F32), -vis_ref[1, rows, :].astype(F32)), start)
            at = block * 2 * LANES
            for line in range(lines):
                into = slice(line * A_CHANS, (line + 1) * A_CHANS)
                x_ref[into, at : at + LANES] = value[0].astype(BF16)
                x_ref[into, at + LANES : at + 2 * LANES] = value[1].astype(BF16)
                if line < lines - 1:
                    value = conj_times(value, step)

    def multiply(i, slot):
        rows = pl.ds(pl.multiple_of(i * A_CHANS, A_CHANS), A_CHANS)
        image = jnp.dot(slots[slot][...], col_ref[...], preferred_element_type=F32)
        out_ref[:, rows, :] = (image * scale).astype(BF16).reshape(lines, A_CHANS, M)

    paired(chans // A_CHANS, fill, multiply)


def make_image(vis, place, step_t, start_t, col, lines, total_rows, groups, away):
    blocks = len(vis)
    _, chans, _ = vis[0].shape
    rows = blocks * LANES
    vmem = pl.BlockSpec(memory_space=pltpu.VMEM)
    flops = 2 * lines * chans * 2 * rows * M
    return pl.pallas_call(
        functools.partial(image_kernel, 1.0 / math.sqrt(total_rows), lines, blocks, groups, away),
        out_shape=(jax.ShapeDtypeStruct((lines, chans, M), BF16), TOKEN),
        in_specs=[pl.BlockSpec(memory_space=pltpu.SMEM)] + [vmem] * (3 + blocks),
        out_specs=(vmem, pl.BlockSpec(memory_space=pltpu.SMEM)),
        scratch_shapes=[pltpu.VMEM((lines * A_CHANS, 2 * rows), BF16)] * 2,
        compiler_params=pltpu.CompilerParams(vmem_limit_bytes=VMEM_SMALL),
        cost_estimate=pl.CostEstimate(flops=flops, bytes_accessed=8 << 20, transcendentals=0),
        name="image",
    )(place, step_t, start_t, col, *vis)


def filter_kernel(groups, step, place_ref, filter_ref, *refs):
    image_refs, out_refs, weight_ref = refs[:groups], refs[groups : 2 * groups], refs[-1]
    lines, chans, _ = out_refs[0].shape
    place = place_ref[2]
    for out_block in range(groups):
        rows = pl.ds(pl.multiple_of(lax.rem(place + out_block, groups) * chans, chans), chans)
        for in_block in range(groups):
            at = lax.rem(place + (groups - in_block), groups) * chans
            weight_ref[
                out_block * chans : (out_block + 1) * chans,
                in_block * chans : (in_block + 1) * chans,
            ] = filter_ref[rows, pl.ds(pl.multiple_of(at, chans), chans)]

    def body(i, carry):
        first = i * step
        image = jnp.concatenate(
            [
                jnp.concatenate([ref[first + line] for line in range(step)], 1)
                for ref in image_refs
            ],
            0,
        )
        result = jnp.dot(weight_ref[...], image, preferred_element_type=F32).astype(BF16)
        for block, out_ref in enumerate(out_refs):
            for line in range(step):
                out_ref[first + line] = result[
                    block * chans : (block + 1) * chans, line * M : (line + 1) * M
                ]
        return carry

    lax.fori_loop(0, lines // step, body, 0)


def filter_images(images, place, fg_filter):
    groups = len(images)
    lines, chans, _ = images[0].shape
    step = min(4, lines)
    vmem = pl.BlockSpec(memory_space=pltpu.VMEM)
    return pl.pallas_call(
        functools.partial(filter_kernel, groups, step),
        out_shape=[jax.ShapeDtypeStruct((lines, chans, M), BF16)] * groups,
        in_specs=[pl.BlockSpec(memory_space=pltpu.SMEM)] + [vmem] * (1 + groups),
        out_specs=[vmem] * groups,
        scratch_shapes=[pltpu.VMEM((F, F), BF16)],
        compiler_params=pltpu.CompilerParams(vmem_limit_bytes=VMEM_FILTER),
        cost_estimate=pl.CostEstimate(
            flops=2 * F * F * lines * M, bytes_accessed=18 << 20, transcendentals=0
        ),
        name="filter",
    )(place, fg_filter, *images)


def predict_kernel(scale, groups, away, place_ref, image_ref, col_ref, step_ref, start_ref, keep_ref, send_ref, *slots):
    lines, chans, _ = image_ref.shape
    blocks = 2 * keep_ref.shape[0]
    count = chans // C_CHANS
    base = lax.rem(place_ref[2] + away, groups) * (chans // FINE)

    def rows_of(i):
        return pl.ds(pl.multiple_of(i * C_CHANS, C_CHANS), C_CHANS)

    def multiply(i, slot, block):
        image = image_ref[:, rows_of(i), :].reshape(lines * C_CHANS, M)
        at = slice(block * 2 * LANES, (block + 1) * 2 * LANES)
        slots[slot][...] = jnp.dot(image, col_ref[:, at], preferred_element_type=F32)

    def collect(i, slot, block):
        h_ref = slots[slot]
        rows = rows_of(i)
        for first in range(0, C_CHANS, C_UNIT):
            group = base + i * (C_CHANS // FINE) + first // FINE
            step = phases(step_ref, group, C_UNIT, block)
            start = phases(start_ref, group, C_UNIT, block)
            total = None
            for line in reversed(range(lines)):
                take = slice(line * C_CHANS + first, line * C_CHANS + first + C_UNIT)
                value = (h_ref[take, :LANES], h_ref[take, LANES:])
                if total is None:
                    total = value
                else:
                    moved = times(total, step)
                    total = (moved[0] + value[0], moved[1] + value[1])
            total = times(total, start)
            real, imag = total[0] * scale, total[1] * -scale
            into = pl.ds(pl.multiple_of(i * C_CHANS + first, C_UNIT), C_UNIT)
            if block < blocks // 2:
                keep_ref[block, 0, into, :] = real
                keep_ref[block, 1, into, :] = imag
            else:
                send_ref[block - blocks // 2, 0, into, :] = real.astype(BF16)
                send_ref[block - blocks // 2, 1, into, :] = imag.astype(BF16)

    def body(i, carry):
        for block in range(blocks):
            if block < blocks - 1:
                multiply(i, (block + 1) % len(slots), block + 1)
            else:
                multiply(jnp.minimum(i + 1, count - 1), 0, 0)
            collect(i, block % len(slots), block)
        return carry

    multiply(0, 0, 0)
    lax.fori_loop(0, count, body, 0)


def predict_part(foreground, place, step_t, start_t, col, groups, away):
    lines, chans, _ = foreground.shape
    rows = col.shape[1] // 2
    vmem = pl.BlockSpec(memory_space=pltpu.VMEM)
    flops = 2 * lines * chans * 2 * rows * M
    half = (rows // LANES // 2, 2, chans, LANES)
    return pl.pallas_call(
        functools.partial(predict_kernel, 1.0 / math.sqrt(L * M), groups, away),
        out_shape=(jax.ShapeDtypeStruct(half, F32), jax.ShapeDtypeStruct(half, BF16)),
        in_specs=[pl.BlockSpec(memory_space=pltpu.SMEM)] + [vmem] * 4,
        out_specs=(vmem, vmem),
        scratch_shapes=[pltpu.VMEM((lines * C_CHANS, 2 * LANES), F32)] * C_SLOTS,
        compiler_params=pltpu.CompilerParams(vmem_limit_bytes=VMEM_SMALL),
        cost_estimate=pl.CostEstimate(flops=flops, bytes_accessed=8 << 20, transcendentals=0),
        name="predict",
    )(place, foreground, col, step_t, start_t)


def local(visibility, flags, u_index, v_index, fg_filter):
    groups, tiles = lax.axis_size("chan"), lax.axis_size("tile")
    chan, tile = lax.axis_index("chan"), lax.axis_index("tile")
    chans = visibility.shape[2]
    total_rows = u_index.shape[0]
    lines = L // (groups * tiles)
    masks = chip_masks(tiles)

    weight = flags.astype(BF16)
    own = jnp.transpose(visibility * weight[:, None, :], (1, 2, 0))
    seen = [own] + [chan_shift(own, groups, away) for away in range(1, groups)]
    place = jnp.stack([tile, (chan * tiles + tile) * lines, chan])
    step_t, start_t, predict_col, image_col, token = tables(u_index, v_index, place, tiles)
    images, tokens = [], [token]
    for away in range(groups):
        block = seen[away]
        if away:
            block = after(block, tokens[min(away - 1, 1)])
        pieces = [tile_swap(block, tiles, mask) for mask in masks[1:]]
        blocks = [block, *pieces]
        if away != 1:
            pieces = lax.optimization_barrier((*pieces, tokens[min(away, 2)]))[:-1]
        blocks += [tile_swap(piece, tiles, 1) for piece in (block, *pieces)]
        image, token = make_image(
            blocks, place, step_t, start_t, image_col, lines, total_rows, groups, away
        )
        images.append(image)
        tokens.append(token)
    foreground = filter_images(images, place, fg_filter)

    parts, first_halves, second_halves = [], [], []
    for turn, away in enumerate(list(range(1, groups)) + [0]):
        here = place
        if turn >= 2:
            here = after(here, first_halves[turn - 2])
        if turn >= 3:
            here = after(here, *second_halves[turn - 3])
        kept, sent = predict_part(
            foreground[away], here, step_t, start_t, predict_col, groups, away
        )
        received = tile_swap(sent, tiles, 1)
        first_halves.append(received)
        total = kept + received.astype(F32)
        received = [
            tile_swap(total[spot].astype(BF16), tiles, mask)
            for spot, mask in enumerate(masks)
            if mask
        ]
        second_halves.append(received)
        part = total[0] + functools.reduce(jnp.add, [piece.astype(F32) for piece in received])
        if away:
            part = chan_shift(part.astype(BF16), groups, away).astype(F32)
        parts.append(part)
    predicted = jnp.transpose(functools.reduce(jnp.add, parts), (2, 0, 1))
    return weight.astype(F32)[:, None, :] * (visibility.astype(F32) - predicted)


def solution(mesh):
    return jax.shard_map(
        local,
        mesh=mesh,
        in_specs=(P("tile", None, "chan"), P("tile", "chan"), P(), P(), P()),
        out_specs=P("tile", None, "chan"),
        check_vma=False,
    )
```

```python
import functools
import math

import jax
import jax.numpy as jnp
from jax import lax
from jax.experimental import pallas as pl
from jax.experimental.pallas import tpu as pltpu
from jax.sharding import PartitionSpec as P

F = 1024
L = 512
M = 256

TWO_PI = 2.0 * math.pi
FINE = 8
DIGIT = 16
GROUPS = F // FINE
LANES = 128
A_CHANS = 16
C_CHANS = 64
C_UNIT = 16
C_SLOTS = 2
VMEM_SMALL = 8 << 20
VMEM_FILTER = 16 << 20
F32 = jnp.float32
BF16 = jnp.bfloat16


def chip_masks(tiles):
    return [mask for mask in range(0, tiles, 2)]


def tile_swap(block, tiles, mask):
    return lax.ppermute(block, "tile", [(t, t ^ mask) for t in range(tiles)])


def chan_shift(block, groups, away):
    return lax.ppermute(block, "chan", [(c, (c + away) % groups) for c in range(groups)])


def wrapped(value, count):
    return jnp.where(value >= count, value - count, value)


def after(value, *others):
    return lax.optimization_barrier((value, *others))[0]


def times(a, b):
    return a[0] * b[0] - a[1] * b[1], a[1] * b[0] + a[0] * b[1]


def conj_times(a, b):
    return a[0] * b[0] + a[1] * b[1], a[1] * b[0] - a[0] * b[1]


def turn_unit(turns, period):
    angle = (turns & (period - 1)).astype(F32) * (TWO_PI / period)
    return jnp.cos(angle), jnp.sin(angle)


def row_of(pair, row, height):
    return tuple(jnp.broadcast_to(part[row : row + 1], (height, LANES)) for part in pair)


def table_kernel(lines, tiles, u_ref, v_ref, step_c, step_f, start_c, start_f, col_ref, turned_ref):
    tile = lax.axis_index("tile")
    first_line = (lax.axis_index("chan") * tiles + tile) * lines
    ids = lax.broadcasted_iota(jnp.int32, (DIGIT, LANES), 0)
    spots = lax.broadcasted_iota(jnp.int32, (tiles, LANES), 0)
    masks = chip_masks(tiles)
    u_all = jnp.zeros((tiles, LANES), jnp.int32)
    for block, mask in enumerate(masks + [mask ^ 1 for mask in masks]):
        source = pl.ds(tile ^ mask, FINE, stride=0)
        u_row, v_row = u_ref[source, :], v_ref[source, :]
        u_all = jnp.where(spots == block, jnp.concatenate([u_row] * (tiles // FINE), 0), u_all)
        step_f[0, block], step_f[1, block] = turn_unit(u_row * ids[:FINE], F * L)
        scaled = u_row * first_line
        start_f[0, block], start_f[1, block] = turn_unit(scaled * ids[:FINE], F * L)
        deep = jnp.concatenate([v_row] * (DIGIT // FINE), 0)
        high = turn_unit(deep * (DIGIT * ids), 2 * M)
        low = turn_unit(deep * ids, 2 * M)
        rows = []
        for row in range(M // DIGIT):
            both = times(row_of(high, row, DIGIT), low)
            rows.append(jnp.concatenate(both, 1).astype(BF16))
        at = slice(block * 2 * LANES, (block + 1) * 2 * LANES)
        whole = jnp.concatenate(rows, 0)
        col_ref[:, at] = whole
        turned_ref[at, :] = whole.T
    for scaled, coarse_ref in ((u_all, step_c), (u_all * first_line, start_c)):
        low = [turn_unit(scaled * (FINE * d), F * L) for d in range(DIGIT)]
        for row in range(GROUPS // DIGIT):
            high = turn_unit(scaled * (F + FINE * DIGIT * row), F * L)
            for d in range(DIGIT):
                coarse_ref[row * DIGIT + d] = jnp.concatenate(times(high, low[d]), 0)


def tables(u_index, v_index, lines, tiles):
    rows = u_index.shape[0]
    vmem = pl.BlockSpec(memory_space=pltpu.VMEM)
    coarse = jax.ShapeDtypeStruct((GROUPS, 2 * tiles, LANES), F32)
    fine = jax.ShapeDtypeStruct((2, tiles, FINE, LANES), F32)
    return pl.pallas_call(
        functools.partial(table_kernel, lines, tiles),
        out_shape=(
            coarse,
            fine,
            coarse,
            fine,
            jax.ShapeDtypeStruct((M, 2 * rows), BF16),
            jax.ShapeDtypeStruct((2 * rows, M), BF16),
        ),
        in_specs=[vmem, vmem],
        out_specs=(vmem,) * 6,
        compiler_params=pltpu.CompilerParams(vmem_limit_bytes=VMEM_SMALL),
        cost_estimate=pl.CostEstimate(flops=3 << 30, bytes_accessed=4 << 20, transcendentals=0),
        name="tables",
    )(u_index.reshape(tiles, LANES), v_index.reshape(tiles, LANES))


def phases(coarse_ref, fine_ref, group, chans, block):
    fine = (fine_ref[0, block], fine_ref[1, block])
    tiles = fine_ref.shape[1]
    parts = []
    for step in range(chans // FINE):
        coarse = [
            coarse_ref[group + step, pl.ds(part * tiles + block, FINE, stride=0), :]
            for part in range(2)
        ]
        parts.append(times(coarse, fine))
    return (
        jnp.concatenate([part[0] for part in parts], 0),
        jnp.concatenate([part[1] for part in parts], 0),
    )


def paired(count, first, second):
    first(0, 0)

    def body(pair, carry):
        first(2 * pair + 1, 1)
        second(2 * pair, 0)
        first(jnp.minimum(2 * pair + 2, count - 1), 0)
        second(2 * pair + 1, 1)
        return carry

    lax.fori_loop(0, count // 2, body, 0)


def image_kernel(scale, lines, blocks, groups, away, step_c, step_f, start_c, start_f, col_ref, *refs):
    vis_refs, out_ref, slots = refs[:blocks], refs[blocks], refs[blocks + 1 :]
    chans = out_ref.shape[1]
    base = wrapped(lax.axis_index("chan") + (groups - away), groups) * (chans // FINE)

    def fill(i, slot):
        x_ref = slots[slot]
        rows = pl.ds(pl.multiple_of(i * A_CHANS, A_CHANS), A_CHANS)
        group = base + i * (A_CHANS // FINE)
        for block in range(blocks):
            step = phases(step_c, step_f, group, A_CHANS, block)
            start = phases(start_c, start_f, group, A_CHANS, block)
            vis_ref = vis_refs[block]
            value = conj_times((vis_ref[0, rows, :].astype(F32), -vis_ref[1, rows, :].astype(F32)), start)
            at = block * 2 * LANES
            for line in range(lines):
                into = slice(line * A_CHANS, (line + 1) * A_CHANS)
                x_ref[into, at : at + LANES] = value[0].astype(BF16)
                x_ref[into, at + LANES : at + 2 * LANES] = value[1].astype(BF16)
                if line < lines - 1:
                    value = conj_times(value, step)

    def multiply(i, slot):
        rows = pl.ds(pl.multiple_of(i * A_CHANS, A_CHANS), A_CHANS)
        image = jnp.dot(slots[slot][...], col_ref[...], preferred_element_type=F32)
        out_ref[:, rows, :] = (image * scale).astype(BF16).reshape(lines, A_CHANS, M)

    paired(chans // A_CHANS, fill, multiply)


def make_image(vis, phase_t, col, lines, total_rows, groups, away):
    blocks = len(vis)
    _, chans, _ = vis[0].shape
    rows = blocks * LANES
    vmem = pl.BlockSpec(memory_space=pltpu.VMEM)
    flops = 4 * lines * chans * 2 * rows * M
    return pl.pallas_call(
        functools.partial(image_kernel, 1.0 / math.sqrt(total_rows), lines, blocks, groups, away),
        out_shape=jax.ShapeDtypeStruct((lines, chans, M), BF16),
        in_specs=[vmem] * (5 + blocks),
        out_specs=vmem,
        scratch_shapes=[pltpu.VMEM((lines * A_CHANS, 2 * rows), BF16)] * 2,
        compiler_params=pltpu.CompilerParams(vmem_limit_bytes=VMEM_SMALL),
        cost_estimate=pl.CostEstimate(flops=flops, bytes_accessed=8 << 20, transcendentals=0),
        name="image",
    )(*phase_t, col, *vis)


def filter_kernel(groups, step, filter_ref, *refs):
    image_refs, out_refs, weight_ref = refs[:groups], refs[groups : 2 * groups], refs[-1]
    lines, chans, _ = out_refs[0].shape
    place = lax.axis_index("chan")
    for out_block in range(groups):
        rows = pl.ds(pl.multiple_of(wrapped(place + out_block, groups) * chans, chans), chans)
        for in_block in range(groups):
            at = wrapped(place + (groups - in_block), groups) * chans
            weight_ref[
                out_block * chans : (out_block + 1) * chans,
                in_block * chans : (in_block + 1) * chans,
            ] = filter_ref[rows, pl.ds(pl.multiple_of(at, chans), chans)]

    def body(i, carry):
        first = i * step
        image = jnp.concatenate(
            [
                jnp.concatenate([ref[first + line] for line in range(step)], 1)
                for ref in image_refs
            ],
            0,
        )
        result = jnp.dot(weight_ref[...], image, preferred_element_type=F32).astype(BF16)
        for block, out_ref in enumerate(out_refs):
            for line in range(step):
                out_ref[first + line] = result[
                    block * chans : (block + 1) * chans, line * M : (line + 1) * M
                ]
        return carry

    lax.fori_loop(0, lines // step, body, 0)


def filter_images(images, fg_filter):
    groups = len(images)
    lines, chans, _ = images[0].shape
    step = min(4, lines)
    vmem = pl.BlockSpec(memory_space=pltpu.VMEM)
    return pl.pallas_call(
        functools.partial(filter_kernel, groups, step),
        out_shape=[jax.ShapeDtypeStruct((lines, chans, M), BF16)] * groups,
        in_specs=[vmem] * (1 + groups),
        out_specs=[vmem] * groups,
        scratch_shapes=[pltpu.VMEM((F, F), BF16)],
        compiler_params=pltpu.CompilerParams(vmem_limit_bytes=VMEM_FILTER),
        cost_estimate=pl.CostEstimate(
            flops=2 * F * F * lines * M, bytes_accessed=18 << 20, transcendentals=0
        ),
        name="filter",
    )(fg_filter, *images)


def predict_kernel(scale, groups, away, image_ref, col_ref, step_c, step_f, start_c, start_f, keep_ref, send_ref, *slots):
    lines, chans, _ = image_ref.shape
    blocks = 2 * keep_ref.shape[0]
    count = chans // C_CHANS
    base = wrapped(lax.axis_index("chan") + away, groups) * (chans // FINE)

    def rows_of(i):
        return pl.ds(pl.multiple_of(i * C_CHANS, C_CHANS), C_CHANS)

    def multiply(i, slot, block):
        image = image_ref[:, rows_of(i), :].reshape(lines * C_CHANS, M)
        at = slice(block * 2 * LANES, (block + 1) * 2 * LANES)
        slots[slot][...] = jnp.dot(image, col_ref[:, at], preferred_element_type=F32)

    def collect(i, slot, block):
        h_ref = slots[slot]
        rows = rows_of(i)
        for first in range(0, C_CHANS, C_UNIT):
            group = base + i * (C_CHANS // FINE) + first // FINE
            step = phases(step_c, step_f, group, C_UNIT, block)
            start = phases(start_c, start_f, group, C_UNIT, block)
            total = None
            for line in reversed(range(lines)):
                take = slice(line * C_CHANS + first, line * C_CHANS + first + C_UNIT)
                value = (h_ref[take, :LANES], h_ref[take, LANES:])
                if total is None:
                    total = value
                else:
                    moved = times(total, step)
                    total = (moved[0] + value[0], moved[1] + value[1])
            total = times(total, start)
            real, imag = total[0] * scale, total[1] * -scale
            into = pl.ds(pl.multiple_of(i * C_CHANS + first, C_UNIT), C_UNIT)
            if block < blocks // 2:
                keep_ref[block, 0, into, :] = real
                keep_ref[block, 1, into, :] = imag
            else:
                send_ref[block - blocks // 2, 0, into, :] = real.astype(BF16)
                send_ref[block - blocks // 2, 1, into, :] = imag.astype(BF16)

    def body(i, carry):
        for block in range(blocks):
            if block < blocks - 1:
                multiply(i, (block + 1) % len(slots), block + 1)
            else:
                multiply(jnp.minimum(i + 1, count - 1), 0, 0)
            collect(i, block % len(slots), block)
        return carry

    multiply(0, 0, 0)
    lax.fori_loop(0, count, body, 0)


def predict_part(foreground, phase_t, col, groups, away):
    lines, chans, _ = foreground.shape
    rows = col.shape[1] // 2
    vmem = pl.BlockSpec(memory_space=pltpu.VMEM)
    flops = 4 * lines * chans * 2 * rows * M
    half = (rows // LANES // 2, 2, chans, LANES)
    return pl.pallas_call(
        functools.partial(predict_kernel, 1.0 / math.sqrt(L * M), groups, away),
        out_shape=(jax.ShapeDtypeStruct(half, F32), jax.ShapeDtypeStruct(half, BF16)),
        in_specs=[vmem] * 6,
        out_specs=(vmem, vmem),
        scratch_shapes=[pltpu.VMEM((lines * C_CHANS, 2 * LANES), F32)] * C_SLOTS,
        compiler_params=pltpu.CompilerParams(vmem_limit_bytes=VMEM_SMALL),
        cost_estimate=pl.CostEstimate(flops=flops, bytes_accessed=8 << 20, transcendentals=0),
        name="predict",
    )(foreground, col, *phase_t)


def local(visibility, flags, u_index, v_index, fg_filter):
    groups, tiles = lax.axis_size("chan"), lax.axis_size("tile")
    chans = visibility.shape[2]
    total_rows = u_index.shape[0]
    lines = L // (groups * tiles)
    masks = chip_masks(tiles)

    weight = flags.astype(BF16)
    own = jnp.transpose(visibility * weight[:, None, :], (1, 2, 0))
    seen = [own] + [chan_shift(own, groups, away) for away in range(1, groups)]
    *phase_t, predict_col, image_col = tables(u_index, v_index, lines, tiles)
    images = []
    for away in range(groups):
        block = seen[away]
        if away:
            block = after(block, images[min(away, 2) - 2] if away > 1 else phase_t[1])
        pieces = [tile_swap(block, tiles, mask) for mask in masks[1:]]
        blocks = [block, *pieces]
        if away == 0:
            pieces = lax.optimization_barrier((*pieces, phase_t[1]))[:-1]
        if away > 1:
            pieces = lax.optimization_barrier((*pieces, images[1]))[:-1]
        blocks += [tile_swap(piece, tiles, 1) for piece in (block, *pieces)]
        images.append(
            make_image(blocks, phase_t, image_col, lines, total_rows, groups, away)
        )
    foreground = filter_images(images, fg_filter)

    parts, first_halves, second_halves = [], [], []
    for turn, away in enumerate(list(range(1, groups)) + [0]):
        here = phase_t
        if turn >= 2:
            here = [*here[:3], after(here[3], first_halves[turn - 2])]
        if turn >= 3:
            here = [*here[:3], after(here[3], *second_halves[turn - 3])]
        kept, sent = predict_part(
            foreground[away], here, predict_col, groups, away
        )
        received = tile_swap(sent, tiles, 1)
        first_halves.append(received)
        total = kept + received.astype(F32)
        received = [
            tile_swap(total[spot].astype(BF16), tiles, mask)
            for spot, mask in enumerate(masks)
            if mask
        ]
        second_halves.append(received)
        part = total[0] + functools.reduce(jnp.add, [piece.astype(F32) for piece in received])
        if away:
            part = chan_shift(part.astype(BF16), groups, away).astype(F32)
        parts.append(part)
    predicted = jnp.transpose(functools.reduce(jnp.add, parts), (2, 0, 1))
    return weight.astype(F32)[:, None, :] * (visibility.astype(F32) - predicted)


def solution(mesh):
    return jax.shard_map(
        local,
        mesh=mesh,
        in_specs=(P("tile", None, "chan"), P("tile", "chan"), P(), P(), P()),
        out_specs=P("tile", None, "chan"),
        check_vma=False,
    )
```

```python
import functools
import math

import jax
import jax.numpy as jnp
from jax import lax
from jax.experimental import pallas as pl
from jax.experimental.pallas import tpu as pltpu
from jax.sharding import PartitionSpec as P

F = 1024
L = 512
M = 256

TWO_PI = 2.0 * math.pi
FINE = 8
DIGIT = 16
GROUPS = F // FINE
LANES = 128
A_CHANS = 16
C_CHANS = 64
C_UNIT = 16
C_SLOTS = 2
VMEM_SMALL = 8 << 20
VMEM_FILTER = 16 << 20
F32 = jnp.float32
BF16 = jnp.bfloat16


def chip_masks(tiles):
    return [mask for mask in range(0, tiles, 2)]


def tile_swap(block, tiles, mask):
    return lax.ppermute(block, "tile", [(t, t ^ mask) for t in range(tiles)])


def chan_shift(block, groups, away):
    return lax.ppermute(block, "chan", [(c, (c + away) % groups) for c in range(groups)])


def wrapped(value, count):
    return jnp.where(value >= count, value - count, value)


def after(value, *others):
    return lax.optimization_barrier((value, *others))[0]


def times(a, b):
    return a[0] * b[0] - a[1] * b[1], a[1] * b[0] + a[0] * b[1]


def conj_times(a, b):
    return a[0] * b[0] + a[1] * b[1], a[1] * b[0] - a[0] * b[1]


def turn_unit(turns, period):
    angle = (turns & (period - 1)).astype(F32) * (TWO_PI / period)
    return jnp.cos(angle), jnp.sin(angle)


def row_of(pair, row, height):
    return tuple(jnp.broadcast_to(part[row : row + 1], (height, LANES)) for part in pair)


def table_kernel(lines, tiles, u_ref, v_ref, step_c, step_f, start_c, start_f, col_ref, turned_ref):
    tile = lax.axis_index("tile")
    first_line = (lax.axis_index("chan") * tiles + tile) * lines
    ids = lax.broadcasted_iota(jnp.int32, (DIGIT, LANES), 0)
    spots = lax.broadcasted_iota(jnp.int32, (tiles, LANES), 0)
    masks = chip_masks(tiles)
    u_all = jnp.zeros((tiles, LANES), jnp.int32)
    for block, mask in enumerate(masks + [mask ^ 1 for mask in masks]):
        source = pl.ds(tile ^ mask, FINE, stride=0)
        u_row, v_row = u_ref[source, :], v_ref[source, :]
        u_all = jnp.where(spots == block, jnp.concatenate([u_row] * (tiles // FINE), 0), u_all)
        step_f[0, block], step_f[1, block] = turn_unit(u_row * ids[:FINE], F * L)
        scaled = u_row * first_line
        start_f[0, block], start_f[1, block] = turn_unit(scaled * ids[:FINE], F * L)
        deep = jnp.concatenate([v_row] * (DIGIT // FINE), 0)
        high = turn_unit(deep * (DIGIT * ids), 2 * M)
        low = turn_unit(deep * ids, 2 * M)
        rows = []
        for row in range(M // DIGIT):
            both = times(row_of(high, row, DIGIT), low)
            rows.append(jnp.concatenate(both, 1).astype(BF16))
        at = slice(block * 2 * LANES, (block + 1) * 2 * LANES)
        whole = jnp.concatenate(rows, 0)
        col_ref[:, at] = whole
        turned_ref[at, :] = whole.T
    for scaled, coarse_ref in ((u_all, step_c), (u_all * first_line, start_c)):
        low = [turn_unit(scaled * (FINE * d), F * L) for d in range(DIGIT)]
        for row in range(GROUPS // DIGIT):
            high = turn_unit(scaled * (F + FINE * DIGIT * row), F * L)
            for d in range(DIGIT):
                coarse_ref[row * DIGIT + d] = jnp.concatenate(times(high, low[d]), 0)


def tables(u_index, v_index, lines, tiles):
    rows = u_index.shape[0]
    vmem = pl.BlockSpec(memory_space=pltpu.VMEM)
    coarse = jax.ShapeDtypeStruct((GROUPS, 2 * tiles, LANES), F32)
    fine = jax.ShapeDtypeStruct((2, tiles, FINE, LANES), F32)
    return pl.pallas_call(
        functools.partial(table_kernel, lines, tiles),
        out_shape=(
            coarse,
            fine,
            coarse,
            fine,
            jax.ShapeDtypeStruct((M, 2 * rows), BF16),
            jax.ShapeDtypeStruct((2 * rows, M), BF16),
        ),
        in_specs=[vmem, vmem],
        out_specs=(vmem,) * 6,
        compiler_params=pltpu.CompilerParams(vmem_limit_bytes=VMEM_SMALL),
        cost_estimate=pl.CostEstimate(flops=3 << 30, bytes_accessed=4 << 20, transcendentals=0),
        name="tables",
    )(u_index.reshape(tiles, LANES), v_index.reshape(tiles, LANES))


def phases(coarse_ref, fine_ref, group, chans, block):
    fine = (fine_ref[0, block], fine_ref[1, block])
    tiles = fine_ref.shape[1]
    parts = []
    for step in range(chans // FINE):
        coarse = [
            coarse_ref[group + step, pl.ds(part * tiles + block, FINE, stride=0), :]
            for part in range(2)
        ]
        parts.append(times(coarse, fine))
    return (
        jnp.concatenate([part[0] for part in parts], 0),
        jnp.concatenate([part[1] for part in parts], 0),
    )


def paired(count, first, second):
    first(0, 0)

    def body(pair, carry):
        first(2 * pair + 1, 1)
        second(2 * pair, 0)
        first(jnp.minimum(2 * pair + 2, count - 1), 0)
        second(2 * pair + 1, 1)
        return carry

    lax.fori_loop(0, count // 2, body, 0)


def image_kernel(scale, lines, blocks, groups, away, step_c, step_f, start_c, start_f, col_ref, *refs):
    vis_refs, out_ref, slots = refs[:blocks], refs[blocks], refs[blocks + 1 :]
    chans = out_ref.shape[1]
    base = wrapped(lax.axis_index("chan") + (groups - away), groups) * (chans // FINE)

    def fill(i, slot):
        x_ref = slots[slot]
        rows = pl.ds(pl.multiple_of(i * A_CHANS, A_CHANS), A_CHANS)
        group = base + i * (A_CHANS // FINE)
        for block in range(blocks):
            step = phases(step_c, step_f, group, A_CHANS, block)
            start = phases(start_c, start_f, group, A_CHANS, block)
            vis_ref = vis_refs[block]
            value = conj_times((vis_ref[0, rows, :].astype(F32), -vis_ref[1, rows, :].astype(F32)), start)
            at = block * 2 * LANES
            for line in range(lines):
                into = slice(line * A_CHANS, (line + 1) * A_CHANS)
                x_ref[into, at : at + LANES] = value[0].astype(BF16)
                x_ref[into, at + LANES : at + 2 * LANES] = value[1].astype(BF16)
                if line < lines - 1:
                    value = conj_times(value, step)

    def multiply(i, slot):
        rows = pl.ds(pl.multiple_of(i * A_CHANS, A_CHANS), A_CHANS)
        image = jnp.dot(slots[slot][...], col_ref[...], preferred_element_type=F32)
        out_ref[:, rows, :] = (image * scale).astype(BF16).reshape(lines, A_CHANS, M)

    paired(chans // A_CHANS, fill, multiply)


def make_image(vis, phase_t, col, lines, total_rows, groups, away):
    blocks = len(vis)
    _, chans, _ = vis[0].shape
    rows = blocks * LANES
    vmem = pl.BlockSpec(memory_space=pltpu.VMEM)
    flops = 4 * lines * chans * 2 * rows * M
    return pl.pallas_call(
        functools.partial(image_kernel, 1.0 / math.sqrt(total_rows), lines, blocks, groups, away),
        out_shape=jax.ShapeDtypeStruct((lines, chans, M), BF16),
        in_specs=[vmem] * (5 + blocks),
        out_specs=vmem,
        scratch_shapes=[pltpu.VMEM((lines * A_CHANS, 2 * rows), BF16)] * 2,
        compiler_params=pltpu.CompilerParams(vmem_limit_bytes=VMEM_SMALL),
        cost_estimate=pl.CostEstimate(flops=flops, bytes_accessed=8 << 20, transcendentals=0),
        name="image",
    )(*phase_t, col, *vis)


def filter_kernel(groups, step, filter_ref, *refs):
    image_refs, out_refs, weight_ref = refs[:groups], refs[groups : 2 * groups], refs[-1]
    lines, chans, _ = out_refs[0].shape
    place = lax.axis_index("chan")
    for out_block in range(groups):
        rows = pl.ds(pl.multiple_of(wrapped(place + out_block, groups) * chans, chans), chans)
        for in_block in range(groups):
            at = wrapped(place + (groups - in_block), groups) * chans
            weight_ref[
                out_block * chans : (out_block + 1) * chans,
                in_block * chans : (in_block + 1) * chans,
            ] = filter_ref[rows, pl.ds(pl.multiple_of(at, chans), chans)]

    def body(i, carry):
        first = i * step
        image = jnp.concatenate(
            [
                jnp.concatenate([ref[first + line] for line in range(step)], 1)
                for ref in image_refs
            ],
            0,
        )
        result = jnp.dot(weight_ref[...], image, preferred_element_type=F32).astype(BF16)
        for block, out_ref in enumerate(out_refs):
            for line in range(step):
                out_ref[first + line] = result[
                    block * chans : (block + 1) * chans, line * M : (line + 1) * M
                ]
        return carry

    lax.fori_loop(0, lines // step, body, 0)


def filter_images(images, fg_filter):
    groups = len(images)
    lines, chans, _ = images[0].shape
    step = min(4, lines)
    vmem = pl.BlockSpec(memory_space=pltpu.VMEM)
    return pl.pallas_call(
        functools.partial(filter_kernel, groups, step),
        out_shape=[jax.ShapeDtypeStruct((lines, chans, M), BF16)] * groups,
        in_specs=[vmem] * (1 + groups),
        out_specs=[vmem] * groups,
        scratch_shapes=[pltpu.VMEM((F, F), BF16)],
        compiler_params=pltpu.CompilerParams(vmem_limit_bytes=VMEM_FILTER),
        cost_estimate=pl.CostEstimate(
            flops=2 * F * F * lines * M, bytes_accessed=18 << 20, transcendentals=0
        ),
        name="filter",
    )(fg_filter, *images)


def predict_kernel(scale, groups, away, image_ref, col_ref, step_c, step_f, start_c, start_f, keep_ref, send_ref, *slots):
    lines, chans, _ = image_ref.shape
    blocks = 2 * keep_ref.shape[0]
    count = chans // C_CHANS
    base = wrapped(lax.axis_index("chan") + away, groups) * (chans // FINE)

    def rows_of(i):
        return pl.ds(pl.multiple_of(i * C_CHANS, C_CHANS), C_CHANS)

    def multiply(i, slot, block):
        image = image_ref[:, rows_of(i), :].reshape(lines * C_CHANS, M)
        at = slice(block * 2 * LANES, (block + 1) * 2 * LANES)
        slots[slot][...] = jnp.dot(image, col_ref[:, at], preferred_element_type=F32)

    def collect(i, slot, block):
        h_ref = slots[slot]
        rows = rows_of(i)
        for first in range(0, C_CHANS, C_UNIT):
            group = base + i * (C_CHANS // FINE) + first // FINE
            step = phases(step_c, step_f, group, C_UNIT, block)
            start = phases(start_c, start_f, group, C_UNIT, block)
            total = None
            for line in reversed(range(lines)):
                take = slice(line * C_CHANS + first, line * C_CHANS + first + C_UNIT)
                value = (h_ref[take, :LANES], h_ref[take, LANES:])
                if total is None:
                    total = value
                else:
                    moved = times(total, step)
                    total = (moved[0] + value[0], moved[1] + value[1])
            total = times(total, start)
            real, imag = total[0] * scale, total[1] * -scale
            into = pl.ds(pl.multiple_of(i * C_CHANS + first, C_UNIT), C_UNIT)
            if block < blocks // 2:
                keep_ref[block, 0, into, :] = real
                keep_ref[block, 1, into, :] = imag
            else:
                send_ref[block - blocks // 2, 0, into, :] = real.astype(BF16)
                send_ref[block - blocks // 2, 1, into, :] = imag.astype(BF16)

    def body(i, carry):
        for block in range(blocks):
            if block < blocks - 1:
                multiply(i, (block + 1) % len(slots), block + 1)
            else:
                multiply(jnp.minimum(i + 1, count - 1), 0, 0)
            collect(i, block % len(slots), block)
        return carry

    multiply(0, 0, 0)
    lax.fori_loop(0, count, body, 0)


def predict_part(foreground, phase_t, col, groups, away):
    lines, chans, _ = foreground.shape
    rows = col.shape[1] // 2
    vmem = pl.BlockSpec(memory_space=pltpu.VMEM)
    flops = 4 * lines * chans * 2 * rows * M
    half = (rows // LANES // 2, 2, chans, LANES)
    return pl.pallas_call(
        functools.partial(predict_kernel, 1.0 / math.sqrt(L * M), groups, away),
        out_shape=(jax.ShapeDtypeStruct(half, F32), jax.ShapeDtypeStruct(half, BF16)),
        in_specs=[vmem] * 6,
        out_specs=(vmem, vmem),
        scratch_shapes=[pltpu.VMEM((lines * C_CHANS, 2 * LANES), F32)] * C_SLOTS,
        compiler_params=pltpu.CompilerParams(vmem_limit_bytes=VMEM_SMALL),
        cost_estimate=pl.CostEstimate(flops=flops, bytes_accessed=8 << 20, transcendentals=0),
        name="predict",
    )(foreground, col, *phase_t)


def local(visibility, flags, u_index, v_index, fg_filter):
    groups, tiles = lax.axis_size("chan"), lax.axis_size("tile")
    chans = visibility.shape[2]
    total_rows = u_index.shape[0]
    lines = L // (groups * tiles)
    masks = chip_masks(tiles)

    weight = flags.astype(BF16)
    own = jnp.transpose(visibility * weight[:, None, :], (1, 2, 0))
    seen = [own] + [chan_shift(own, groups, away) for away in range(1, groups)]
    *phase_t, predict_col, image_col = tables(u_index, v_index, lines, tiles)
    images = []
    for away in range(groups):
        block = seen[away]
        if away:
            block = after(block, images[min(away, 2) - 2] if away > 1 else phase_t[1])
        pieces = [tile_swap(block, tiles, mask) for mask in masks[1:]]
        blocks = [block, *pieces]
        if away == 0:
            pieces = lax.optimization_barrier((*pieces, phase_t[1]))[:-1]
        else:
            pieces = lax.optimization_barrier((*pieces, images[min(away, 2) - 1]))[:-1]
        blocks += [tile_swap(piece, tiles, 1) for piece in (block, *pieces)]
        images.append(
            make_image(blocks, phase_t, image_col, lines, total_rows, groups, away)
        )
    foreground = filter_images(images, fg_filter)

    parts, first_halves, second_halves, passed_on = [], [], [], []
    for turn, away in enumerate(list(range(1, groups)) + [0]):
        waits = []
        if turn >= 2:
            waits.append(first_halves[turn - 2])
        if turn >= 3:
            waits += second_halves[turn - 3]
        if turn == groups - 1:
            waits += passed_on[turn - 1]
        here = [*phase_t[:3], after(phase_t[3], *waits)] if waits else phase_t
        kept, sent = predict_part(foreground[away], here, predict_col, groups, away)
        if turn == groups - 1:
            sent = after(sent, *second_halves[turn - 1])
        received = tile_swap(sent, tiles, 1)
        first_halves.append(received)
        total = kept + received.astype(F32)
        passed_on.append([total[spot].astype(BF16) for spot in range(1, len(masks))])
        received = [
            tile_swap(piece, tiles, mask) for piece, mask in zip(passed_on[turn], masks[1:])
        ]
        second_halves.append(received)
        part = total[0] + functools.reduce(jnp.add, [piece.astype(F32) for piece in received])
        if away:
            part = chan_shift(part.astype(BF16), groups, away).astype(F32)
        parts.append(part)
    predicted = jnp.transpose(functools.reduce(jnp.add, parts), (2, 0, 1))
    return weight.astype(F32)[:, None, :] * (visibility.astype(F32) - predicted)


def solution(mesh):
    return jax.shard_map(
        local,
        mesh=mesh,
        in_specs=(P("tile", None, "chan"), P("tile", "chan"), P(), P(), P()),
        out_specs=P("tile", None, "chan"),
        check_vma=False,
    )
```

```python
import functools
import math

import jax
import jax.numpy as jnp
from jax import lax
from jax.experimental import pallas as pl
from jax.experimental.pallas import tpu as pltpu
from jax.sharding import PartitionSpec as P

F = 1024
L = 512
M = 256

TWO_PI = 2.0 * math.pi
FINE = 8
DIGIT = 16
GROUPS = F // FINE
LANES = 128
A_CHANS = 16
C_CHANS = 64
C_UNIT = 16
C_SLOTS = 2
VMEM_SMALL = 8 << 20
VMEM_FILTER = 16 << 20
F32 = jnp.float32
BF16 = jnp.bfloat16


def chip_masks(tiles):
    return [0] + sorted(range(2, tiles, 2), key=lambda mask: -mask.bit_count())


def tile_swap(block, tiles, mask):
    return lax.ppermute(block, "tile", [(t, t ^ mask) for t in range(tiles)])


def chan_shift(block, groups, away):
    return lax.ppermute(block, "chan", [(c, (c + away) % groups) for c in range(groups)])


def wrapped(value, count):
    return jnp.where(value >= count, value - count, value)


def after(value, *others):
    return lax.optimization_barrier((value, *others))[0]


def times(a, b):
    return a[0] * b[0] - a[1] * b[1], a[1] * b[0] + a[0] * b[1]


def conj_times(a, b):
    return a[0] * b[0] + a[1] * b[1], a[1] * b[0] - a[0] * b[1]


def turn_unit(turns, period):
    angle = (turns & (period - 1)).astype(F32) * (TWO_PI / period)
    return jnp.cos(angle), jnp.sin(angle)


def row_of(pair, row, height):
    return tuple(jnp.broadcast_to(part[row : row + 1], (height, LANES)) for part in pair)


def table_kernel(lines, tiles, u_ref, v_ref, step_c, step_f, start_c, start_f, col_ref, turned_ref):
    tile = lax.axis_index("tile")
    first_line = (lax.axis_index("chan") * tiles + tile) * lines
    ids = lax.broadcasted_iota(jnp.int32, (DIGIT, LANES), 0)
    spots = lax.broadcasted_iota(jnp.int32, (tiles, LANES), 0)
    masks = chip_masks(tiles)
    u_all = jnp.zeros((tiles, LANES), jnp.int32)
    for block, mask in enumerate(masks + [mask ^ 1 for mask in masks]):
        source = pl.ds(tile ^ mask, FINE, stride=0)
        u_row, v_row = u_ref[source, :], v_ref[source, :]
        u_all = jnp.where(spots == block, jnp.concatenate([u_row] * (tiles // FINE), 0), u_all)
        step_f[0, block], step_f[1, block] = turn_unit(u_row * ids[:FINE], F * L)
        scaled = u_row * first_line
        start_f[0, block], start_f[1, block] = turn_unit(scaled * ids[:FINE], F * L)
        deep = jnp.concatenate([v_row] * (DIGIT // FINE), 0)
        high = turn_unit(deep * (DIGIT * ids), 2 * M)
        low = turn_unit(deep * ids, 2 * M)
        rows = []
        for row in range(M // DIGIT):
            both = times(row_of(high, row, DIGIT), low)
            rows.append(jnp.concatenate(both, 1).astype(BF16))
        at = slice(block * 2 * LANES, (block + 1) * 2 * LANES)
        whole = jnp.concatenate(rows, 0)
        col_ref[:, at] = whole
        turned_ref[at, :] = whole.T
    for scaled, coarse_ref in ((u_all, step_c), (u_all * first_line, start_c)):
        low = [turn_unit(scaled * (FINE * d), F * L) for d in range(DIGIT)]
        for row in range(GROUPS // DIGIT):
            high = turn_unit(scaled * (F + FINE * DIGIT * row), F * L)
            for d in range(DIGIT):
                coarse_ref[row * DIGIT + d] = jnp.concatenate(times(high, low[d]), 0)


def tables(u_index, v_index, lines, tiles):
    rows = u_index.shape[0]
    vmem = pl.BlockSpec(memory_space=pltpu.VMEM)
    coarse = jax.ShapeDtypeStruct((GROUPS, 2 * tiles, LANES), F32)
    fine = jax.ShapeDtypeStruct((2, tiles, FINE, LANES), F32)
    return pl.pallas_call(
        functools.partial(table_kernel, lines, tiles),
        out_shape=(
            coarse,
            fine,
            coarse,
            fine,
            jax.ShapeDtypeStruct((M, 2 * rows), BF16),
            jax.ShapeDtypeStruct((2 * rows, M), BF16),
        ),
        in_specs=[vmem, vmem],
        out_specs=(vmem,) * 6,
        compiler_params=pltpu.CompilerParams(vmem_limit_bytes=VMEM_SMALL),
        cost_estimate=pl.CostEstimate(flops=3 << 30, bytes_accessed=4 << 20, transcendentals=0),
        name="tables",
    )(u_index.reshape(tiles, LANES), v_index.reshape(tiles, LANES))


def phases(coarse_ref, fine_ref, group, chans, block):
    fine = (fine_ref[0, block], fine_ref[1, block])
    tiles = fine_ref.shape[1]
    parts = []
    for step in range(chans // FINE):
        coarse = [
            coarse_ref[group + step, pl.ds(part * tiles + block, FINE, stride=0), :]
            for part in range(2)
        ]
        parts.append(times(coarse, fine))
    return (
        jnp.concatenate([part[0] for part in parts], 0),
        jnp.concatenate([part[1] for part in parts], 0),
    )


def paired(count, first, second):
    first(0, 0)

    def body(pair, carry):
        first(2 * pair + 1, 1)
        second(2 * pair, 0)
        first(jnp.minimum(2 * pair + 2, count - 1), 0)
        second(2 * pair + 1, 1)
        return carry

    lax.fori_loop(0, count // 2, body, 0)


def image_kernel(scale, lines, blocks, groups, away, step_c, step_f, start_c, start_f, col_ref, *refs):
    vis_refs, out_ref, slots = refs[:blocks], refs[blocks], refs[blocks + 1 :]
    chans = out_ref.shape[1]
    base = wrapped(lax.axis_index("chan") + (groups - away), groups) * (chans // FINE)

    def fill(i, slot):
        x_ref = slots[slot]
        rows = pl.ds(pl.multiple_of(i * A_CHANS, A_CHANS), A_CHANS)
        group = base + i * (A_CHANS // FINE)
        for block in range(blocks):
            step = phases(step_c, step_f, group, A_CHANS, block)
            start = phases(start_c, start_f, group, A_CHANS, block)
            vis_ref = vis_refs[block]
            value = conj_times((vis_ref[0, rows, :].astype(F32), -vis_ref[1, rows, :].astype(F32)), start)
            at = block * 2 * LANES
            for line in range(lines):
                into = slice(line * A_CHANS, (line + 1) * A_CHANS)
                x_ref[into, at : at + LANES] = value[0].astype(BF16)
                x_ref[into, at + LANES : at + 2 * LANES] = value[1].astype(BF16)
                if line < lines - 1:
                    value = conj_times(value, step)

    def multiply(i, slot):
        rows = pl.ds(pl.multiple_of(i * A_CHANS, A_CHANS), A_CHANS)
        image = jnp.dot(slots[slot][...], col_ref[...], preferred_element_type=F32)
        out_ref[:, rows, :] = (image * scale).astype(BF16).reshape(lines, A_CHANS, M)

    paired(chans // A_CHANS, fill, multiply)


def make_image(vis, phase_t, col, lines, total_rows, groups, away):
    blocks = len(vis)
    _, chans, _ = vis[0].shape
    rows = blocks * LANES
    vmem = pl.BlockSpec(memory_space=pltpu.VMEM)
    flops = 4 * lines * chans * 2 * rows * M
    return pl.pallas_call(
        functools.partial(image_kernel, 1.0 / math.sqrt(total_rows), lines, blocks, groups, away),
        out_shape=jax.ShapeDtypeStruct((lines, chans, M), BF16),
        in_specs=[vmem] * (5 + blocks),
        out_specs=vmem,
        scratch_shapes=[pltpu.VMEM((lines * A_CHANS, 2 * rows), BF16)] * 2,
        compiler_params=pltpu.CompilerParams(vmem_limit_bytes=VMEM_SMALL),
        cost_estimate=pl.CostEstimate(flops=flops, bytes_accessed=8 << 20, transcendentals=0),
        name="image",
    )(*phase_t, col, *vis)


def filter_kernel(groups, step, filter_ref, *refs):
    image_refs, out_refs, weight_ref = refs[:groups], refs[groups : 2 * groups], refs[-1]
    lines, chans, _ = out_refs[0].shape
    place = lax.axis_index("chan")
    for out_block in range(groups):
        rows = pl.ds(pl.multiple_of(wrapped(place + out_block, groups) * chans, chans), chans)
        for in_block in range(groups):
            at = wrapped(place + (groups - in_block), groups) * chans
            weight_ref[
                out_block * chans : (out_block + 1) * chans,
                in_block * chans : (in_block + 1) * chans,
            ] = filter_ref[rows, pl.ds(pl.multiple_of(at, chans), chans)]

    def body(i, carry):
        first = i * step
        image = jnp.concatenate(
            [
                jnp.concatenate([ref[first + line] for line in range(step)], 1)
                for ref in image_refs
            ],
            0,
        )
        result = jnp.dot(weight_ref[...], image, preferred_element_type=F32).astype(BF16)
        for block, out_ref in enumerate(out_refs):
            for line in range(step):
                out_ref[first + line] = result[
                    block * chans : (block + 1) * chans, line * M : (line + 1) * M
                ]
        return carry

    lax.fori_loop(0, lines // step, body, 0)


def filter_images(images, fg_filter):
    groups = len(images)
    lines, chans, _ = images[0].shape
    step = min(4, lines)
    vmem = pl.BlockSpec(memory_space=pltpu.VMEM)
    return pl.pallas_call(
        functools.partial(filter_kernel, groups, step),
        out_shape=[jax.ShapeDtypeStruct((lines, chans, M), BF16)] * groups,
        in_specs=[vmem] * (1 + groups),
        out_specs=[vmem] * groups,
        scratch_shapes=[pltpu.VMEM((F, F), BF16)],
        compiler_params=pltpu.CompilerParams(vmem_limit_bytes=VMEM_FILTER),
        cost_estimate=pl.CostEstimate(
            flops=2 * F * F * lines * M, bytes_accessed=18 << 20, transcendentals=0
        ),
        name="filter",
    )(fg_filter, *images)


def predict_kernel(scale, groups, away, image_ref, col_ref, step_c, step_f, start_c, start_f, keep_ref, send_ref, *slots):
    lines, chans, _ = image_ref.shape
    blocks = 2 * keep_ref.shape[0]
    count = chans // C_CHANS
    base = wrapped(lax.axis_index("chan") + away, groups) * (chans // FINE)

    def rows_of(i):
        return pl.ds(pl.multiple_of(i * C_CHANS, C_CHANS), C_CHANS)

    def multiply(i, slot, block):
        image = image_ref[:, rows_of(i), :].reshape(lines * C_CHANS, M)
        at = slice(block * 2 * LANES, (block + 1) * 2 * LANES)
        slots[slot][...] = jnp.dot(image, col_ref[:, at], preferred_element_type=F32)

    def collect(i, slot, block):
        h_ref = slots[slot]
        rows = rows_of(i)
        for first in range(0, C_CHANS, C_UNIT):
            group = base + i * (C_CHANS // FINE) + first // FINE
            step = phases(step_c, step_f, group, C_UNIT, block)
            start = phases(start_c, start_f, group, C_UNIT, block)
            total = None
            for line in reversed(range(lines)):
                take = slice(line * C_CHANS + first, line * C_CHANS + first + C_UNIT)
                value = (h_ref[take, :LANES], h_ref[take, LANES:])
                if total is None:
                    total = value
                else:
                    moved = times(total, step)
                    total = (moved[0] + value[0], moved[1] + value[1])
            total = times(total, start)
            real, imag = total[0] * scale, total[1] * -scale
            into = pl.ds(pl.multiple_of(i * C_CHANS + first, C_UNIT), C_UNIT)
            if block < blocks // 2:
                keep_ref[block, 0, into, :] = real
                keep_ref[block, 1, into, :] = imag
            else:
                send_ref[block - blocks // 2, 0, into, :] = real.astype(BF16)
                send_ref[block - blocks // 2, 1, into, :] = imag.astype(BF16)

    def body(i, carry):
        for block in range(blocks):
            if block < blocks - 1:
                multiply(i, (block + 1) % len(slots), block + 1)
            else:
                multiply(jnp.minimum(i + 1, count - 1), 0, 0)
            collect(i, block % len(slots), block)
        return carry

    multiply(0, 0, 0)
    lax.fori_loop(0, count, body, 0)


def predict_part(foreground, phase_t, col, groups, away):
    lines, chans, _ = foreground.shape
    rows = col.shape[1] // 2
    vmem = pl.BlockSpec(memory_space=pltpu.VMEM)
    flops = 4 * lines * chans * 2 * rows * M
    half = (rows // LANES // 2, 2, chans, LANES)
    return pl.pallas_call(
        functools.partial(predict_kernel, 1.0 / math.sqrt(L * M), groups, away),
        out_shape=(jax.ShapeDtypeStruct(half, F32), jax.ShapeDtypeStruct(half, BF16)),
        in_specs=[vmem] * 6,
        out_specs=(vmem, vmem),
        scratch_shapes=[pltpu.VMEM((lines * C_CHANS, 2 * LANES), F32)] * C_SLOTS,
        compiler_params=pltpu.CompilerParams(vmem_limit_bytes=VMEM_SMALL),
        cost_estimate=pl.CostEstimate(flops=flops, bytes_accessed=8 << 20, transcendentals=0),
        name="predict",
    )(foreground, col, *phase_t)


def local(visibility, flags, u_index, v_index, fg_filter):
    groups, tiles = lax.axis_size("chan"), lax.axis_size("tile")
    chans = visibility.shape[2]
    total_rows = u_index.shape[0]
    lines = L // (groups * tiles)
    masks = chip_masks(tiles)

    weight = flags.astype(BF16)
    own = jnp.transpose(visibility * weight[:, None, :], (1, 2, 0))
    seen = [own] + [chan_shift(own, groups, away) for away in range(1, groups)]
    *phase_t, predict_col, image_col = tables(u_index, v_index, lines, tiles)
    images = []
    for away in range(groups):
        block = seen[away]
        if away:
            block = after(block, images[min(away, 2) - 2] if away > 1 else phase_t[1])
        pieces = [tile_swap(block, tiles, mask) for mask in masks[1:]]
        blocks = [block, *pieces]
        if away == 0:
            pieces = lax.optimization_barrier((*pieces, phase_t[1]))[:-1]
        else:
            pieces = lax.optimization_barrier((*pieces, images[min(away, 2) - 1]))[:-1]
        blocks += [tile_swap(piece, tiles, 1) for piece in (block, *pieces)]
        images.append(
            make_image(blocks, phase_t, image_col, lines, total_rows, groups, away)
        )
    foreground = filter_images(images, fg_filter)

    parts, first_halves, second_halves, passed_on = [], [], [], []
    for turn, away in enumerate(list(range(1, groups)) + [0]):
        waits = []
        if turn >= 2:
            waits.append(first_halves[turn - 2])
        if turn >= 3:
            waits += second_halves[turn - 3]
        if turn == groups - 1:
            waits += passed_on[turn - 1]
        here = [*phase_t[:3], after(phase_t[3], *waits)] if waits else phase_t
        kept, sent = predict_part(foreground[away], here, predict_col, groups, away)
        if turn == groups - 1:
            sent = after(sent, *second_halves[turn - 1])
        received = tile_swap(sent, tiles, 1)
        first_halves.append(received)
        total = kept + received.astype(F32)
        passed_on.append([total[spot].astype(BF16) for spot in range(1, len(masks))])
        received = [
            tile_swap(piece, tiles, mask) for piece, mask in zip(passed_on[turn], masks[1:])
        ]
        second_halves.append(received)
        part = total[0] + functools.reduce(jnp.add, [piece.astype(F32) for piece in received])
        if away:
            part = chan_shift(part.astype(BF16), groups, away).astype(F32)
        parts.append(part)
    predicted = jnp.transpose(functools.reduce(jnp.add, parts), (2, 0, 1))
    return weight.astype(F32)[:, None, :] * (visibility.astype(F32) - predicted)


def solution(mesh):
    return jax.shard_map(
        local,
        mesh=mesh,
        in_specs=(P("tile", None, "chan"), P("tile", "chan"), P(), P(), P()),
        out_specs=P("tile", None, "chan"),
        check_vma=False,
    )
```
